128 devices in a mesh: row: 8 (over y, core), col: 16 (over x, z).
Axes of the slice: x: 4, y: 4, z: 4, core: 2. Of those that a mesh axis runs over, the one named last changes fastest.
Arguments:
- alignment: bfloat16 [128, 768, 256], P('row', 'col'), may hold values from -6.5 to 6.5
- pair_features: float32 [768, 768, 128], P('row', 'col'), may hold values from -6 to 6
- query_weight: bfloat16 [256, 256], replicated, may hold values from -25 to 25
- key_weight: bfloat16 [256, 256], replicated, may hold values from -0.375 to 0.375
- value_projection: bfloat16 [256, 256], replicated, may hold values from -0.375 to 0.375
- gate_projection: bfloat16 [256, 256], replicated, may hold values from -0.375 to 0.375
- gate_bias: float32 [256], replicated, may hold values from -4 to 4
- output_projection: bfloat16 [256, 256], replicated, may hold values from -0.375 to 0.375
- left_projection: bfloat16 [256, 32], replicated, may hold values from -0.375 to 0.375
- right_projection: bfloat16 [256, 32], replicated, may hold values from -0.375 to 0.375
- outer_weight: bfloat16 [1024, 128], replicated, may hold values from -0.75 to 0.75
- outer_bias: float32 [128], replicated, may hold values from -3 to 3
- expand_weight: bfloat16 [128, 512], replicated, may hold values from -0.5 to 0.5
- shrink_weight: bfloat16 [512, 128], replicated, may hold values from -0.25 to 0.25
- cotangent: float32 [768, 768, 128], P('row', 'col'), may hold values from -6 to 6
Outputs:
- updated: bfloat16 [128, 768, 256], P('row', 'col')
- pair_out: float32 [768, 768, 128], P('row', 'col')
- grad_left: float32 [128, 24576], P('col', 'row')
- grad_right: float32 [128, 24576], P('row', 'col')
The draws below stay inside these ranges and needn't reach their ends.
All inputs are finite; a program needn't handle non-finite values.
Results may differ from the reference program's by a relative error of at most 0.017.
Values may be sent and summed in bfloat16 or wider, within the bound.
A program may use at most 192 MiB of HBM per device.

```python
import jax
import jax.numpy as jnp
from jax import lax

ENTRY_FEATURES = 256
ATTENTION_HEADS = 8
HEAD_WIDTH = 32
FACTOR_WIDTH = 32
PAIR_W = 128
TRANSITION = 512
SEQUENCE_COUNT = 128
RESIDUE_COUNT = 768


def shared_base(key):
    base_random_key = jax.random.normal(jax.random.fold_in(key, 7), (ENTRY_FEATURES, ATTENTION_HEADS * HEAD_WIDTH), jnp.float32)
    return jnp.clip(base_random_key, -6.0, 6.0) * ENTRY_FEATURES ** (-0.5)


def draw_key_weight(key, part):
    return shared_base(key).astype(jnp.bfloat16)


def draw_query_weight(key, part):
    fresh_random_sample = jax.random.normal(jax.random.fold_in(key, 8), (ENTRY_FEATURES, ATTENTION_HEADS * HEAD_WIDTH), jnp.float32)
    fresh_random_sample = jnp.clip(fresh_random_sample, -6.0, 6.0) * ENTRY_FEATURES ** (-0.5)
    return fresh_random_sample.astype(jnp.bfloat16)


def draw_alignment(key, part):
    value_rows = jnp.clip(jax.random.normal(jax.random.fold_in(key, 5), (SEQUENCE_COUNT, RESIDUE_COUNT, ENTRY_FEATURES), jnp.float32), -6.0, 6.0)
    return value_rows.astype(jnp.bfloat16)


def block_levels(rng, dims, split, smallest, high):
    def one(dim, blocks):
        steps = jax.random.uniform(jax.random.fold_in(jax.random.fold_in(rng, 6), dim), (blocks,), jnp.float32, smallest / len(split), high / len(split))
        return jnp.repeat(jnp.exp(steps), dims[dim] // blocks).reshape((-1,) + (1,) * (len(dims) - dim - 1))

    level = one(*split[0])
    for cut in split[1:]:
        level = level * one(*cut)
    return level


def gaussian(own_key, dims, scale, bound, pieces=(), held_as=jnp.bfloat16):
    entries = jax.random.normal(own_key, dims, jnp.float32) * scale
    if len(pieces) > 0:
        entries = block_levels(own_key, dims, pieces, -0.22, 0.18) * entries
    return jnp.clip(entries, min=-bound, max=bound).astype(held_as)


def setup_inputs(seed: int = 0) -> dict:
    splits = jax.random.split(jax.random.key(seed), 16)
    return {
        "alignment": draw_alignment(jax.random.fold_in(splits[15], 71), 0),
        "pair_features": gaussian(splits[1], (RESIDUE_COUNT, RESIDUE_COUNT, PAIR_W), 1.0, 6.0, ((0, 8), (1, 16)), jnp.float32),
        "query_weight": draw_query_weight(jax.random.fold_in(splits[15], 71), 0),
        "key_weight": draw_key_weight(jax.random.fold_in(splits[15], 71), 0),
        "value_projection": gaussian(splits[4], (ENTRY_FEATURES, ATTENTION_HEADS * HEAD_WIDTH), ENTRY_FEATURES ** -0.5, 0.375),
        "gate_projection": gaussian(splits[5], (ENTRY_FEATURES, ATTENTION_HEADS * HEAD_WIDTH), ENTRY_FEATURES ** -0.5, 0.375),
        "gate_bias": gaussian(splits[6], (ATTENTION_HEADS * HEAD_WIDTH,), 1.0, 4.0, (), jnp.float32),
        "output_projection": gaussian(splits[7], (ATTENTION_HEADS * HEAD_WIDTH, ENTRY_FEATURES), (ATTENTION_HEADS * HEAD_WIDTH) ** -0.5, 0.375),
        "left_projection": gaussian(splits[8], (ENTRY_FEATURES, FACTOR_WIDTH), ENTRY_FEATURES ** -0.5, 0.375),
        "right_projection": gaussian(splits[9], (ENTRY_FEATURES, FACTOR_WIDTH), ENTRY_FEATURES ** -0.5, 0.375),
        "outer_weight": gaussian(splits[10], (FACTOR_WIDTH * FACTOR_WIDTH, PAIR_W), (2 * FACTOR_WIDTH) ** -0.5, 0.75),
        "outer_bias": gaussian(splits[11], (PAIR_W,), 0.5, 3.0, (), jnp.float32),
        "expand_weight": gaussian(splits[12], (PAIR_W, TRANSITION), PAIR_W ** -0.5, 0.5),
        "shrink_weight": gaussian(splits[13], (TRANSITION, PAIR_W), TRANSITION ** -0.5, 0.25),
        "cotangent": gaussian(splits[14], (RESIDUE_COUNT, RESIDUE_COUNT, PAIR_W), 1.0, 6.0, ((0, 8), (1, 16)), jnp.float32),
    }


epsilon = 1e-05

def layer_normalise(value_rows):
    value_rows = value_rows.astype(jnp.float32)
    average = lax.optimization_barrier(jnp.mean(value_rows, axis=-1, keepdims=True))
    centred = value_rows - average
    variance = lax.optimization_barrier(jnp.mean(centred * centred, axis=-1, keepdims=True))
    return centred * lax.rsqrt(variance + epsilon)

def gelu_value(before):
    return 0.5 * before * (1.0 + lax.erf(before * 0.7071067811865476))

def gelu_slope(before):
    return 0.5 * (1.0 + lax.erf(before * 0.7071067811865476)) + before * jnp.exp(-0.5 * before * before) * 0.3989422804014327

def dot_last(left_side, right_side):
    return lax.dot_general(left_side, right_side, (((1,), (1,)), ((), ())), preferred_element_type=jnp.float32)

def transition(middle, cotangent, expand_weight, shrink_weight):
    average = lax.optimization_barrier(jnp.mean(middle, axis=-1, keepdims=True))
    centred = middle - average
    variance = lax.optimization_barrier(jnp.mean(centred * centred, axis=-1, keepdims=True))
    inverse = lax.rsqrt(variance + epsilon)
    spread = centred * inverse
    before = jnp.dot(spread.astype(jnp.bfloat16), expand_weight, preferred_element_type=jnp.float32)
    hidden = gelu_value(before).astype(jnp.bfloat16)
    result = middle + jnp.dot(hidden, shrink_weight, preferred_element_type=jnp.float32)
    back_hidden = dot_last(cotangent.astype(jnp.bfloat16), shrink_weight)
    back_before = (back_hidden * gelu_slope(before)).astype(jnp.bfloat16)
    back_spread = dot_last(back_before, expand_weight)
    centre_term = lax.optimization_barrier(jnp.mean(back_spread, axis=-1, keepdims=True))
    slope_term = lax.optimization_barrier(jnp.mean(back_spread * spread, axis=-1, keepdims=True))
    back_middle = cotangent + inverse * (back_spread - centre_term - spread * slope_term)
    return (result, back_middle)

def column_attend(column_block, query_weight, key_weight, value_projection, gate_projection, gate_bias, output_projection):
    seq_count, res_count, feat_width = column_block.shape
    flat_rows = layer_normalise(column_block).astype(jnp.bfloat16).reshape(seq_count * res_count, feat_width)
    head_shape = (seq_count, res_count, ATTENTION_HEADS, HEAD_WIDTH)
    query_proj = jnp.dot(flat_rows, query_weight, preferred_element_type=jnp.float32).astype(jnp.bfloat16).reshape(head_shape)
    key_proj = jnp.dot(flat_rows, key_weight, preferred_element_type=jnp.float32).astype(jnp.bfloat16).reshape(head_shape)
    value_proj = jnp.dot(flat_rows, value_projection, preferred_element_type=jnp.float32).astype(jnp.bfloat16).reshape(head_shape)
    gating = jax.nn.sigmoid(jnp.dot(flat_rows, gate_projection, preferred_element_type=jnp.float32) + gate_bias).reshape(head_shape)
    scores = jnp.einsum('srhc,trhc->rhst', query_proj.astype(jnp.float32), key_proj.astype(jnp.float32)) * HEAD_WIDTH ** (-0.5)
    highest = lax.optimization_barrier(jnp.max(scores, axis=-1, keepdims=True))
    raised = jnp.exp(scores - highest)
    totals = lax.optimization_barrier(jnp.sum(raised, axis=-1))
    rounded = lax.optimization_barrier(raised.astype(jnp.bfloat16)).astype(jnp.float32)
    blended = jnp.einsum('rhst,trhc->srhc', rounded, value_proj.astype(jnp.float32))
    blended = blended / jnp.transpose(totals, (2, 0, 1))[..., None]
    gated_out = (gating * blended).astype(jnp.bfloat16).reshape(seq_count * res_count, ATTENTION_HEADS * HEAD_WIDTH)
    update = jnp.dot(gated_out, output_projection, preferred_element_type=jnp.float32).reshape(column_block.shape)
    return (column_block.astype(jnp.float32) + update).astype(jnp.bfloat16)

def reference(alignment, pair_features, query_weight, key_weight, value_projection, gate_projection, gate_bias, output_projection, left_projection, right_projection, outer_weight, outer_bias, expand_weight, shrink_weight, cotangent):
    width_of_block = 16
    count_of_blocks = RESIDUE_COUNT // width_of_block
    split_into_blocks = jnp.transpose(alignment.reshape(SEQUENCE_COUNT, count_of_blocks, width_of_block, ENTRY_FEATURES), (1, 0, 2, 3))

    def attend_block(column_block):
        return column_attend(column_block, query_weight, key_weight, value_projection, gate_projection, gate_bias, output_projection)
    attended_rows = lax.map(attend_block, split_into_blocks)
    updated = jnp.transpose(attended_rows, (1, 0, 2, 3)).reshape(SEQUENCE_COUNT, RESIDUE_COUNT, ENTRY_FEATURES)
    factor_row_matrix = layer_normalise(updated).astype(jnp.bfloat16).reshape(SEQUENCE_COUNT * RESIDUE_COUNT, ENTRY_FEATURES)
    left_factors = jnp.dot(factor_row_matrix, left_projection, preferred_element_type=jnp.float32).astype(jnp.bfloat16).reshape(SEQUENCE_COUNT, RESIDUE_COUNT, FACTOR_WIDTH)
    right_factors = jnp.dot(factor_row_matrix, right_projection, preferred_element_type=jnp.float32).astype(jnp.bfloat16).reshape(SEQUENCE_COUNT, RESIDUE_COUNT, FACTOR_WIDTH)
    right_wide = right_factors.astype(jnp.float32)
    scaling = 1.0 / SEQUENCE_COUNT

    def one_block(carried, block_index):
        left_part = lax.dynamic_slice_in_dim(left_factors, block_index * width_of_block, width_of_block, 1).astype(jnp.float32)
        pair_part = lax.dynamic_slice_in_dim(pair_features, block_index * width_of_block, width_of_block, 0)
        cot_part = lax.dynamic_slice_in_dim(cotangent, block_index * width_of_block, width_of_block, 0)
        outer_tile = (jnp.einsum('sic,sje->ijce', left_part, right_wide) * scaling).astype(jnp.bfloat16)
        outer_tile = outer_tile.reshape(width_of_block * RESIDUE_COUNT, FACTOR_WIDTH * FACTOR_WIDTH)
        middle = pair_part.reshape(width_of_block * RESIDUE_COUNT, PAIR_W) + jnp.dot(outer_tile, outer_weight, preferred_element_type=jnp.float32) + outer_bias
        result, back_middle = transition(middle, cot_part.reshape(width_of_block * RESIDUE_COUNT, PAIR_W), expand_weight, shrink_weight)
        back_outer = dot_last(back_middle.astype(jnp.bfloat16), outer_weight).astype(jnp.bfloat16)
        back_outer = back_outer.reshape(width_of_block, RESIDUE_COUNT, FACTOR_WIDTH, FACTOR_WIDTH).astype(jnp.float32)
        grad_part = jnp.einsum('ijce,sje->sic', back_outer, right_wide).reshape(SEQUENCE_COUNT, width_of_block * FACTOR_WIDTH) * scaling
        carried = carried + jnp.einsum('ijce,sic->sje', back_outer, left_part).reshape(SEQUENCE_COUNT, RESIDUE_COUNT * FACTOR_WIDTH) * scaling
        return (carried, (result.reshape(width_of_block, RESIDUE_COUNT, PAIR_W), grad_part))
    indices = jnp.arange(count_of_blocks, dtype=jnp.int32)
    start_grad = jnp.zeros((SEQUENCE_COUNT, RESIDUE_COUNT * FACTOR_WIDTH), jnp.float32)
    grad_right, (pair_blocks, grad_blocks) = lax.scan(one_block, start_grad, indices)
    pair_out = pair_blocks.reshape(RESIDUE_COUNT, RESIDUE_COUNT, PAIR_W)
    grad_left = jnp.transpose(grad_blocks, (1, 0, 2)).reshape(SEQUENCE_COUNT, RESIDUE_COUNT * FACTOR_WIDTH)
    return (updated, pair_out, grad_left, grad_right)
```

```python
import functools

import jax
import jax.numpy as jnp
from jax import lax
from jax.experimental import pallas as pl
from jax.experimental.pallas import tpu as pltpu
from jax.sharding import PartitionSpec as P

HEADS = 8
HEAD_W = 32
FACTOR = 32
PAIR_W = 128
EPS = 1e-05
F32 = jnp.float32
BF16 = jnp.bfloat16


def dot_nn(a, b):
    return jnp.dot(a, b, preferred_element_type=F32)


def dot_nt(a, b):
    return lax.dot_general(a, b, (((1,), (1,)), ((), ())), preferred_element_type=F32)


def mean_last(x):
    return jnp.mean(x, axis=-1, keepdims=True)


def transition(middle, cot, expand, shrink):
    average = mean_last(middle)
    centred = middle - average
    variance = mean_last(centred * centred)
    inverse = lax.rsqrt(variance + EPS)
    spread = centred * inverse
    before = dot_nn(spread.astype(BF16), expand)
    cdf = 0.5 * (1.0 + lax.erf(before * 0.7071067811865476))
    hidden = (before * cdf).astype(BF16)
    result = middle + dot_nn(hidden, shrink)
    slope = cdf + before * jnp.exp(-0.5 * before * before) * 0.3989422804014327
    back_hidden = dot_nt(cot.astype(BF16), shrink)
    back_before = (back_hidden * slope).astype(BF16)
    back_spread = dot_nt(back_before, expand)
    centre = mean_last(back_spread)
    along = mean_last(back_spread * spread)
    back = cot + inverse * (back_spread - centre - spread * along)
    return result, back


def pair_kernel(
    lt_ref, rt_ref, w_ref, bias_ref, expand_ref, shrink_ref, pf_ref, ct_ref,
    out_ref, gl_ref, gr_ref,
    wbd, r2, osc, mid, bmsc, bsc,
):
    n_i = 32
    n_g = n_i // 4
    n_j = 48

    @pl.when(pl.program_id(0) == 0)
    def _():
        wbd[...] = jnp.zeros_like(wbd)
        for e in range(FACTOR):
            for q in range(4):
                wbd[pl.ds(e * 128 + q * 32, 32), pl.ds(q * 128, 128)] = w_ref[e]
        rows = lax.broadcasted_iota(jnp.int32, (128, 128), 0)
        cols = lax.broadcasted_iota(jnp.int32, (128, 128), 1)
        eye = jnp.where(rows == cols, 1.0, 0.0).astype(BF16)
        r2[...] = dot_nt(eye, rt_ref[...]).astype(BF16)
        gr_ref[...] = jnp.zeros_like(gr_ref)

    lt = lt_ref[...].reshape(n_i * FACTOR, 128)

    @pl.loop(0, 4)
    def _(eb):
        o = dot_nt(rt_ref[pl.ds(pl.multiple_of(eb * 384, 384), 384), :], lt).astype(BF16)
        for e in range(8):
            for g in range(n_g):
                osc[pl.ds(g * n_j, n_j), pl.ds(pl.multiple_of(eb * 1024 + e * 128, 128), 128)] = o[
                    e * n_j : (e + 1) * n_j, g * 128 : (g + 1) * 128
                ]

    mid[...] = dot_nn(osc[...], wbd[...])

    @pl.loop(0, n_g)
    def _(g):
        rows = pl.ds(pl.multiple_of(g * n_j, n_j), n_j)
        block = mid[rows, :]
        x = jnp.concatenate([block[:, q * 128 : (q + 1) * 128] for q in range(4)], axis=0)
        pf = pf_ref[pl.ds(g * 2, 2)].reshape(4 * n_j, PAIR_W)
        ct = ct_ref[pl.ds(g * 2, 2)].reshape(4 * n_j, PAIR_W)
        x = pf + x + bias_ref[...]
        result, back = transition(x, ct, expand_ref[...], shrink_ref[...])
        out_ref[pl.ds(g * 2, 2)] = result.reshape(2, 2, n_j, PAIR_W)
        back = back.astype(BF16)
        for q in range(4):
            bmsc[rows, pl.ds(q * 128, 128)] = back[q * n_j : (q + 1) * n_j, :]

    @pl.loop(0, 4)
    def _(eb):
        b = dot_nt(bmsc[...], wbd[pl.ds(pl.multiple_of(eb * 1024, 1024), 1024), :]).astype(BF16)
        for e in range(8):
            for g in range(n_g):
                bsc[pl.ds(pl.multiple_of(eb * 384 + e * n_j, n_j), n_j), pl.ds(g * 128, 128)] = b[
                    g * n_j : (g + 1) * n_j, e * 128 : (e + 1) * 128
                ]

    gl_ref[...] = dot_nn(r2[...], bsc[...]).astype(BF16)
    gr_ref[...] += dot_nn(bsc[...], lt)


def pair_call(lt, rt, w, bias, expand, shrink, pf, ct):
    lt = lt.reshape(16, 6, 32, 128)
    pf = pf.reshape(16, 6, 48, 128)
    ct = ct.reshape(16, 6, 48, 128)
    whole = lambda shape: pl.BlockSpec(shape, lambda q: (0,) * len(shape))
    chunk = lambda d: pl.BlockSpec((16, 2, d, 128), lambda q: (0, q, 0, 0))
    out, gl, gr = pl.pallas_call(
        pair_kernel,
        grid=(3,),
        in_specs=[
            chunk(32), whole((1536, 128)), whole((32, 32, 128)), whole((1, 128)),
            whole((128, 512)), whole((512, 128)), chunk(48), chunk(48),
        ],
        out_specs=[chunk(48), pl.BlockSpec((128, 1024), lambda q: (0, q)), whole((1536, 128))],
        out_shape=[
            jax.ShapeDtypeStruct((16, 6, 48, 128), F32),
            jax.ShapeDtypeStruct((128, 3072), BF16),
            jax.ShapeDtypeStruct((1536, 128), F32),
        ],
        scratch_shapes=[
            pltpu.VMEM((4096, 512), BF16),
            pltpu.VMEM((128, 1536), BF16),
            pltpu.VMEM((384, 4096), BF16),
            pltpu.VMEM((384, 512), F32),
            pltpu.VMEM((384, 512), BF16),
            pltpu.VMEM((1536, 1024), BF16),
        ],
        compiler_params=pltpu.CompilerParams(
            dimension_semantics=("arbitrary",), vmem_limit_bytes=56 * 1024 * 1024
        ),
        name="pair",
    )(lt, rt, w, bias, expand, shrink, pf, ct)
    return out.reshape(96, 48, 128), gl, gr


def layer_normalise(x):
    x = x.astype(F32)
    average = mean_last(x)
    centred = x - average
    variance = mean_last(centred * centred)
    return centred * lax.rsqrt(variance + EPS)


def column_attend(block, wq, wk, wv, wg, gate_bias, wo):
    seqs, res, feats = block.shape
    rows = layer_normalise(block).astype(BF16).reshape(seqs * res, feats)
    head_shape = (seqs, res, HEADS, HEAD_W)
    q = dot_nn(rows, wq).astype(BF16).reshape(head_shape)
    k = dot_nn(rows, wk).astype(BF16).reshape(head_shape)
    v = dot_nn(rows, wv).astype(BF16).reshape(head_shape)
    gating = jax.nn.sigmoid(dot_nn(rows, wg) + gate_bias).reshape(head_shape)
    scores = jnp.einsum("srhc,trhc->rhst", q, k, preferred_element_type=F32) * HEAD_W ** (-0.5)
    highest = jnp.max(scores, axis=-1, keepdims=True)
    raised = jnp.exp(scores - highest)
    totals = jnp.sum(raised, axis=-1)
    blended = jnp.einsum("rhst,trhc->srhc", raised.astype(BF16), v, preferred_element_type=F32)
    blended = blended / jnp.transpose(totals, (2, 0, 1))[..., None]
    gated = (gating * blended).astype(BF16).reshape(seqs * res, HEADS * HEAD_W)
    update = dot_nn(gated, wo).reshape(block.shape)
    return (block.astype(F32) + update).astype(BF16)


def sent_and_summed(x, axis, dim):
    size = lax.axis_size(axis)
    before, after = x.shape[:dim], x.shape[dim + 1 :]
    cut = jnp.moveaxis(x.reshape(*before, size, -1, *after), dim, 0)
    blocks = lax.all_to_all(cut, axis, 0, 0, tiled=True)
    return jnp.sum(blocks.astype(F32), axis=0)


def local(
    alignment, pair_features, query_weight, key_weight, value_projection, gate_projection,
    gate_bias, output_projection, left_projection, right_projection, outer_weight, outer_bias,
    expand_weight, shrink_weight, cotangent,
):
    seqs, res, feats = alignment.shape
    parts = lax.axis_size("row")
    cut = alignment.reshape(seqs, parts, res // parts, feats)
    part_in = lax.all_to_all(cut, "row", split_axis=1, concat_axis=0, tiled=True)
    inner = part_in.reshape(part_in.shape[0], part_in.shape[2], part_in.shape[3])
    attended = column_attend(
        inner, query_weight, key_weight, value_projection, gate_projection, gate_bias,
        output_projection,
    )
    returned = lax.all_to_all(
        attended.reshape(part_in.shape), "row", split_axis=0, concat_axis=1, tiled=True
    )
    updated = returned.reshape(seqs, res, feats)
    rows = layer_normalise(attended).astype(BF16).reshape(-1, feats)
    lr = dot_nn(rows, jnp.concatenate([left_projection, right_projection], axis=1)).astype(BF16)
    lr = lr.reshape(128, 6, 2, FACTOR).transpose(2, 1, 3, 0)
    left = lax.all_gather(lr[0], "row", axis=0, tiled=True)
    right = lax.all_gather(lr[1], "row", axis=0, tiled=True)
    every = lax.all_gather(left, "col")
    mine = lax.axis_index("row") * 2
    lt = lax.dynamic_slice_in_dim(every, mine, 2, 0).reshape(96, FACTOR, 128)
    rt = (right.transpose(1, 0, 2) * (1.0 / 128)).astype(BF16).reshape(1536, 128)
    w = outer_weight.reshape(FACTOR, FACTOR, PAIR_W).transpose(1, 0, 2)
    pair_out, gl, gr = pair_call(
        lt, rt, w, outer_bias.reshape(1, -1), expand_weight, shrink_weight, pair_features, cotangent
    )
    grad_left = sent_and_summed(gl, "col", 0)
    grad_left = grad_left.reshape(8, 3, 16, 64).transpose(0, 2, 1, 3).reshape(8, 3072)
    gr = (gr * (1.0 / 128)).astype(BF16).reshape(FACTOR, 48, 128).transpose(2, 1, 0).reshape(128, 1536)
    grad_right = sent_and_summed(gr, "row", 0)
    return updated, pair_out, grad_left, grad_right


def solution(mesh):
    return jax.shard_map(
        local,
        mesh=mesh,
        in_specs=(P("row", "col", None), P("row", "col", None)) + (P(),) * 12 + (P("row", "col", None),),
        out_specs=(P("row", "col", None), P("row", "col", None), P("col", "row"), P("row", "col")),
        check_vma=False,
    )
```

```python
import jax
import jax.numpy as jnp
from jax import lax
from jax.experimental import pallas as pl
from jax.experimental.pallas import tpu as pltpu
from jax.sharding import PartitionSpec as P

HEADS = 8
HEAD_W = 32
FACTOR = 32
PAIR_W = 128
EPS = 1e-05
F32 = jnp.float32
BF16 = jnp.bfloat16
MESH = pl.DeviceIdType.MESH

ROWS = 8
COLS = 16
SEQ = 128
STAGES = 3
N_J = 48
N_I = 32
N_G = N_I // 4


def dot_nn(a, b):
    return jnp.dot(a, b, preferred_element_type=F32)


def dot_nt(a, b):
    return lax.dot_general(a, b, (((1,), (1,)), ((), ())), preferred_element_type=F32)


def mean_last(x):
    return jnp.mean(x, axis=-1, keepdims=True)


def layer_normalise(x):
    average = mean_last(x)
    centred = x - average
    variance = mean_last(centred * centred)
    return centred * lax.rsqrt(variance + EPS)


def transition(middle, cot, expand, shrink):
    average = mean_last(middle)
    centred = middle - average
    variance = mean_last(centred * centred)
    inverse = lax.rsqrt(variance + EPS)
    spread = centred * inverse
    before = dot_nn(spread.astype(BF16), expand)
    cdf = 0.5 * (1.0 + lax.erf(before * 0.7071067811865476))
    hidden = (before * cdf).astype(BF16)
    result = middle + dot_nn(hidden, shrink)
    slope = cdf + before * jnp.exp(-0.5 * before * before) * 0.3989422804014327
    back_hidden = dot_nt(cot.astype(BF16), shrink)
    back_before = (back_hidden * slope).astype(BF16)
    back_spread = dot_nt(back_before, expand)
    centre = mean_last(back_spread)
    along = mean_last(back_spread * spread)
    back = cot + inverse * (back_spread - centre - spread * along)
    return result, back


def identity(n):
    rows = lax.broadcasted_iota(jnp.int32, (n, n), 0)
    cols = lax.broadcasted_iota(jnp.int32, (n, n), 1)
    return jnp.where(rows == cols, 1.0, 0.0).astype(BF16)


def attend(x, wq, wk, wv, wg, gate_bias, wo):
    flat = x.reshape(2 * SEQ, 256).astype(F32)
    rows = layer_normalise(flat).astype(BF16)
    query = dot_nn(rows, wq).astype(BF16)
    key = dot_nn(rows, wk).astype(BF16)
    value = dot_nn(rows, wv).astype(BF16)
    gating = jax.nn.sigmoid(dot_nn(rows, wg) + gate_bias)
    head_of = lax.broadcasted_iota(jnp.int32, (SEQ, 256), 1) // HEAD_W
    blended = []
    for n in range(2):
        part = slice(n * SEQ, (n + 1) * SEQ)
        q32 = query[part].astype(F32)
        masked = jnp.concatenate(
            [jnp.where(head_of == h, q32, 0.0).astype(BF16) for h in range(HEADS)], axis=0
        )
        scores = dot_nt(masked, key[part]) * HEAD_W ** (-0.5)
        raised = jnp.exp(scores - jnp.max(scores, axis=-1, keepdims=True))
        totals = jnp.sum(raised, axis=-1, keepdims=True)
        mixed = dot_nn(raised.astype(BF16), value[part]) / totals
        total = jnp.zeros((SEQ, 256), F32)
        for h in range(HEADS):
            total = jnp.where(head_of == h, mixed[h * SEQ : (h + 1) * SEQ], total)
        blended.append(total)
    gated = (gating * jnp.concatenate(blended, axis=0)).astype(BF16)
    return (flat + dot_nn(gated, wo)).astype(BF16)


def kernel(
    x_ref, wq, wk, wv, wg, gate_bias, wo, wleft, wright, w_ref, bias_ref, expand_ref, shrink_ref,
    pf_hbm, ct_hbm,
    upd_hbm, out_hbm, gl_ref, gr_ref,
    xbuf, ubuf, proj, lsend, rsend, ltbuf, rtbuf, rtf, rt, r2, wf, wbd,
    pf, ct, out, osc, mid, bmsc, bsc, gacc, glsend, glrecv, grsend, grrecv,
    xs, xr, ls, lr, rs, rr, us, ur, gs, gr_sem, hs, hr, mem,
):
    row = lax.axis_index("row")
    col = lax.axis_index("col")
    owner = col // 2
    diagonal = row == owner
    my_source = lax.rem(col, 2) * ROWS + row

    barrier = pltpu.get_barrier_semaphore()

    @pl.loop(1, ROWS)
    def _(off):
        pl.semaphore_signal(barrier, inc=1, device_id=(lax.rem(row + off, ROWS), col), device_id_type=MESH)

    @pl.loop(1, COLS)
    def _(off):
        pl.semaphore_signal(barrier, inc=1, device_id=(row, lax.rem(col + off, COLS)), device_id_type=MESH)

    @pl.loop(0, 2 * ROWS)
    def _(n):
        r, c = lax.rem(n, ROWS), 2 * row + n // ROWS

        @pl.when(jnp.logical_not(jnp.logical_and(r == row, c == col)))
        def _():
            pl.semaphore_signal(barrier, inc=1, device_id=(r, c), device_id_type=MESH)

    load_pf = pltpu.make_async_copy(pf_hbm, pf, mem.at[0])
    load_ct = pltpu.make_async_copy(ct_hbm, ct, mem.at[1])
    load_pf.start()
    load_ct.start()

    eye = identity(128)
    proj[0:32, :] = dot_nt(eye[:32, :32], wleft[...]).astype(BF16)
    proj[32:64, :] = dot_nt(eye[:32, :32], wright[...]).astype(BF16)
    wf[...] = w_ref[...].astype(F32)
    wbd[...] = jnp.zeros_like(wbd)
    for e in range(FACTOR):
        block = wf[pl.ds(e, FACTOR, stride=FACTOR), :].astype(BF16)
        for q in range(4):
            wbd[pl.ds(e * 128 + q * 32, 32), pl.ds(q * 128, 128)] = block
    gacc[...] = jnp.zeros_like(gacc)

    pl.semaphore_wait(barrier, ROWS - 1 + COLS - 1 + 2 * ROWS - jnp.where(diagonal, 1, 0))

    def x_copy(t, peer, slot):
        return pltpu.make_async_remote_copy(
            src_ref=x_ref.at[pl.ds(6 * peer + 2 * t, 2)],
            dst_ref=xbuf.at[pl.ds(2 * t, 2), pl.ds(pl.multiple_of(16 * slot, 16), 16)],
            send_sem=xs.at[t, peer],
            recv_sem=xr.at[t, slot],
            device_id=(peer, col),
            device_id_type=MESH,
        )

    @pl.loop(0, STAGES)
    def _(t):
        @pl.loop(1, ROWS)
        def _(off):
            x_copy(t, lax.rem(row + off, ROWS), row).start()

        xbuf[pl.ds(2 * t, 2), pl.ds(pl.multiple_of(16 * row, 16), 16)] = x_ref[pl.ds(6 * row + 2 * t, 2)]

    def l_copy(t, target, source):
        return pltpu.make_async_remote_copy(
            src_ref=lsend.at[t],
            dst_ref=ltbuf.at[t, source],
            send_sem=ls.at[t, target],
            recv_sem=lr.at[t, source],
            device_id=(owner, target),
            device_id_type=MESH,
        )

    def r_copy(t, peer, slot):
        return pltpu.make_async_remote_copy(
            src_ref=rsend.at[t],
            dst_ref=rtbuf.at[pl.ds(6 * slot + 2 * t, 2)],
            send_sem=rs.at[t, peer],
            recv_sem=rr.at[t, slot],
            device_id=(peer, col),
            device_id_type=MESH,
        )

    @pl.loop(0, STAGES)
    def _(t):
        @pl.loop(1, ROWS)
        def _(off):
            peer = lax.rem(row + off, ROWS)
            x_copy(t, peer, peer).wait_recv()

        new = attend(
            xbuf[pl.ds(2 * t, 2)], wq[...], wk[...], wv[...], wg[...], gate_bias[...], wo[...]
        )
        ubuf[pl.ds(2 * t, 2)] = new.reshape(2, SEQ, 256)
        factors = dot_nt(proj[...], layer_normalise(new.astype(F32)).astype(BF16))
        left = factors[:32].astype(BF16)
        right = (factors[32:] * (1.0 / SEQ)).astype(BF16)
        for n in range(2):
            lsend[t, n] = left[:, n * SEQ : (n + 1) * SEQ]
            rsend[t, n] = right[:, n * SEQ : (n + 1) * SEQ]

        @pl.loop(1, ROWS)
        def _(off):
            r_copy(t, lax.rem(row + off, ROWS), row).start()

        rtbuf[pl.ds(6 * row + 2 * t, 2)] = rsend[t]

        @pl.when(jnp.logical_not(diagonal))
        def _():
            l_copy(t, col, my_source).start()

        @pl.when(diagonal)
        def _():
            ltbuf[t, my_source] = lsend[t]

        @pl.loop(1, COLS)
        def _(off):
            l_copy(t, lax.rem(col + off, COLS), my_source).start()

    def u_copy(peer, slot):
        return pltpu.make_async_remote_copy(
            src_ref=ubuf.at[:, pl.ds(pl.multiple_of(16 * peer, 16), 16)],
            dst_ref=upd_hbm.at[pl.ds(6 * slot, 6)],
            send_sem=us.at[peer],
            recv_sem=ur.at[slot],
            device_id=(peer, col),
            device_id_type=MESH,
        )

    @pl.loop(1, ROWS)
    def _(off):
        u_copy(lax.rem(row + off, ROWS), row).start()

    own = pltpu.make_async_copy(
        ubuf.at[:, pl.ds(pl.multiple_of(16 * row, 16), 16)], upd_hbm.at[pl.ds(6 * row, 6)], mem.at[2]
    )
    own.start()

    @pl.loop(0, STAGES)
    def _(t):
        @pl.loop(1, ROWS)
        def _(off):
            peer = lax.rem(row + off, ROWS)
            r_copy(t, peer, peer).wait_recv()

    for j in range(N_J):
        rtf[pl.ds(j, FACTOR, stride=N_J), :] = rtbuf[j].astype(F32)
    rt[...] = rtf[...].astype(BF16)
    r2[...] = dot_nt(eye, rt[...]).astype(BF16)
    load_pf.wait()
    load_ct.wait()

    def gl_copy(q, target, source):
        return pltpu.make_async_remote_copy(
            src_ref=glsend.at[q, target],
            dst_ref=glrecv.at[q, source],
            send_sem=gs.at[q, target],
            recv_sem=gr_sem.at[q, source],
            device_id=(row, target),
            device_id_type=MESH,
        )

    def store_copy(q):
        part = (slice(None), pl.ds(2 * q, 2))
        return pltpu.make_async_copy(out.at[part], out_hbm.at[part], mem.at[3 + q])

    @pl.loop(0, STAGES)
    def _(q):
        @pl.loop(0, 2 * ROWS)
        def _(n):
            @pl.when(jnp.logical_not(jnp.logical_and(diagonal, n == my_source)))
            def _():
                l_copy(q, col, n).wait_recv()

        lt = ltbuf[q].reshape(N_I * FACTOR, SEQ)

        @pl.loop(0, 4)
        def _(eb):
            o = dot_nt(rt[pl.ds(pl.multiple_of(eb * 384, 384), 384), :], lt).astype(BF16)
            for e in range(8):
                for g in range(N_G):
                    osc[pl.ds(g * N_J, N_J), pl.ds(pl.multiple_of(eb * 1024 + e * 128, 128), 128)] = o[
                        e * N_J : (e + 1) * N_J, g * 128 : (g + 1) * 128
                    ]

        mid[...] = dot_nn(osc[...], wbd[...])

        @pl.loop(0, N_G)
        def _(g):
            rows = pl.ds(pl.multiple_of(g * N_J, N_J), N_J)
            block = mid[rows, :]
            x = jnp.concatenate([block[:, n * 128 : (n + 1) * 128] for n in range(4)], axis=0)
            part = (pl.ds(g * 2, 2), pl.ds(q * 2, 2))
            cot = ct[part].reshape(4 * N_J, PAIR_W)
            x = pf[part].reshape(4 * N_J, PAIR_W) + x + bias_ref[...]
            result, back = transition(x, cot, expand_ref[...], shrink_ref[...])
            out[part] = result.reshape(2, 2, N_J, PAIR_W)
            back = back.astype(BF16)
            for n in range(4):
                bmsc[rows, pl.ds(n * 128, 128)] = back[n * N_J : (n + 1) * N_J, :]

        store_copy(q).start()

        @pl.loop(0, 4)
        def _(eb):
            b = dot_nt(bmsc[...], wbd[pl.ds(pl.multiple_of(eb * 1024, 1024), 1024), :]).astype(BF16)
            for e in range(8):
                for g in range(N_G):
                    bsc[pl.ds(pl.multiple_of(eb * 384 + e * N_J, N_J), N_J), pl.ds(g * 128, 128)] = b[
                        g * N_J : (g + 1) * N_J, e * 128 : (e + 1) * 128
                    ]

        gl = dot_nn(r2[...], bsc[...])
        for d in range(COLS):
            part = gl[8 * d : 8 * d + 8]
            glsend[q, d] = jnp.concatenate([part[:, :512], part[:, 512:]], axis=0).astype(BF16)

        @pl.loop(1, COLS)
        def _(off):
            gl_copy(q, lax.rem(col + off, COLS), col).start()

        gacc[...] += dot_nn(bsc[...], lt)

    grt = dot_nt(eye, (gacc[...] * (1.0 / SEQ)).astype(BF16)).astype(BF16)
    for d in range(ROWS):
        grsend[d] = grt[16 * d : 16 * d + 16]

    def gr_copy(peer, slot):
        return pltpu.make_async_remote_copy(
            src_ref=grsend.at[peer],
            dst_ref=grrecv.at[slot],
            send_sem=hs.at[peer],
            recv_sem=hr.at[slot],
            device_id=(peer, col),
            device_id_type=MESH,
        )

    @pl.loop(1, ROWS)
    def _(off):
        gr_copy(lax.rem(row + off, ROWS), row).start()

    @pl.loop(0, STAGES)
    def _(q):
        glrecv[q, col] = glsend[q, col]

        @pl.loop(1, COLS)
        def _(off):
            source = lax.rem(col + off, COLS)
            gl_copy(q, source, source).wait_recv()

        total = jnp.zeros((16, 512), F32)
        for s in range(COLS):
            total = total + glrecv[q, s].astype(F32)
        gl_ref[q] = total

    grrecv[row] = grsend[row]

    @pl.loop(1, ROWS)
    def _(off):
        peer = lax.rem(row + off, ROWS)
        gr_copy(peer, peer).wait_recv()
        u_copy(peer, peer).wait_recv()

    total = jnp.zeros((16, N_J * FACTOR), F32)
    for s in range(ROWS):
        total = total + grrecv[s].astype(F32)
    gr_ref[...] = total

    own.wait()

    @pl.loop(1, ROWS)
    def _(off):
        peer = lax.rem(row + off, ROWS)
        u_copy(peer, row).wait_send()
        gr_copy(peer, row).wait_send()

    @pl.loop(0, STAGES)
    def _(t):
        store_copy(t).wait()

        @pl.loop(1, ROWS)
        def _(off):
            peer = lax.rem(row + off, ROWS)
            x_copy(t, peer, row).wait_send()
            r_copy(t, peer, row).wait_send()

        @pl.when(jnp.logical_not(diagonal))
        def _():
            l_copy(t, col, my_source).wait_send()

        @pl.loop(1, COLS)
        def _(off):
            target = lax.rem(col + off, COLS)
            l_copy(t, target, my_source).wait_send()
            gl_copy(t, target, col).wait_send()


def local(
    alignment, pair_features, query_weight, key_weight, value_projection, gate_projection,
    gate_bias, output_projection, left_projection, right_projection, outer_weight, outer_bias,
    expand_weight, shrink_weight, cotangent,
):
    vmem = pl.BlockSpec(memory_space=pltpu.VMEM)
    hbm = pl.BlockSpec(memory_space=pl.ANY)
    dma = pltpu.SemaphoreType.DMA
    upd, out, gl, gr = pl.pallas_call(
        kernel,
        in_specs=[vmem] * 13 + [hbm] * 2,
        out_specs=[hbm, hbm, vmem, vmem],
        out_shape=[
            jax.ShapeDtypeStruct((48, 16, 256), BF16),
            jax.ShapeDtypeStruct((16, 6, N_J, PAIR_W), F32),
            jax.ShapeDtypeStruct((STAGES, 16, 512), F32),
            jax.ShapeDtypeStruct((16, N_J * FACTOR), F32),
        ],
        scratch_shapes=[
            pltpu.VMEM((6, SEQ, 256), BF16),
            pltpu.VMEM((6, SEQ, 256), BF16),
            pltpu.VMEM((64, 256), BF16),
            pltpu.VMEM((STAGES, 2, FACTOR, SEQ), BF16),
            pltpu.VMEM((STAGES, 2, FACTOR, SEQ), BF16),
            pltpu.VMEM((STAGES, 16, 2, FACTOR, SEQ), BF16),
            pltpu.VMEM((N_J, FACTOR, SEQ), BF16),
            pltpu.VMEM((FACTOR * N_J, SEQ), F32),
            pltpu.VMEM((FACTOR * N_J, SEQ), BF16),
            pltpu.VMEM((SEQ, FACTOR * N_J), BF16),
            pltpu.VMEM((FACTOR * FACTOR, PAIR_W), F32),
            pltpu.VMEM((4096, 512), BF16),
            pltpu.VMEM((16, 6, N_J, PAIR_W), F32),
            pltpu.VMEM((16, 6, N_J, PAIR_W), F32),
            pltpu.VMEM((16, 6, N_J, PAIR_W), F32),
            pltpu.VMEM((N_G * N_J, 4096), BF16),
            pltpu.VMEM((N_G * N_J, 512), F32),
            pltpu.VMEM((N_G * N_J, 512), BF16),
            pltpu.VMEM((FACTOR * N_J, 1024), BF16),
            pltpu.VMEM((FACTOR * N_J, SEQ), F32),
            pltpu.VMEM((STAGES, COLS, 16, 512), BF16),
            pltpu.VMEM((STAGES, COLS, 16, 512), BF16),
            pltpu.VMEM((ROWS, 16, N_J * FACTOR), BF16),
            pltpu.VMEM((ROWS, 16, N_J * FACTOR), BF16),
            dma((STAGES, ROWS)), dma((STAGES, ROWS)),
            dma((STAGES, COLS)), dma((STAGES, COLS)),
            dma((STAGES, ROWS)), dma((STAGES, ROWS)),
            dma((ROWS,)), dma((ROWS,)),
            dma((STAGES, COLS)), dma((STAGES, COLS)),
            dma((ROWS,)), dma((ROWS,)),
            dma((6,)),
        ],
        compiler_params=pltpu.CompilerParams(
            collective_id=0, has_side_effects=True, vmem_limit_bytes=60 * 1024 * 1024
        ),
        name="block",
    )(
        alignment.transpose(1, 0, 2), query_weight, key_weight, value_projection, gate_projection,
        gate_bias.reshape(1, -1), output_projection, left_projection, right_projection,
        outer_weight, outer_bias.reshape(1, -1), expand_weight, shrink_weight,
        pair_features.reshape(16, 6, N_J, PAIR_W), cotangent.reshape(16, 6, N_J, PAIR_W),
    )
    grad_left = gl.reshape(STAGES, 2, 8, 8, 64).transpose(2, 1, 3, 0, 4).reshape(8, 3072)
    grad_right = gr.reshape(16, FACTOR, N_J).transpose(0, 2, 1).reshape(16, 1536)
    return upd.transpose(1, 0, 2), out.reshape(96, N_J, PAIR_W), grad_left, grad_right


def solution(mesh):
    return jax.shard_map(
        local,
        mesh=mesh,
        in_specs=(P("row", "col", None), P("row", "col", None)) + (P(),) * 12 + (P("row", "col", None),),
        out_specs=(P("row", "col", None), P("row", "col", None), P("col", "row"), P("row", "col")),
        check_vma=False,
    )
```

```python
import jax
import jax.numpy as jnp
from jax import lax
from jax.experimental import pallas as pl
from jax.experimental.pallas import tpu as pltpu
from jax.sharding import PartitionSpec as P

HEADS = 8
HEAD_W = 32
FACTOR = 32
PAIR_W = 128
EPS = 1e-05
F32 = jnp.float32
BF16 = jnp.bfloat16
MESH = pl.DeviceIdType.MESH
UNROLL = 2

ROWS = 8
COLS = 16
SEQ = 128
STAGES = 3
N_J = 48
N_I = 32
N_G = N_I // 4


def dot_nn(a, b):
    return jnp.dot(a, b, preferred_element_type=F32)


def dot_nt(a, b):
    return lax.dot_general(a, b, (((1,), (1,)), ((), ())), preferred_element_type=F32)


def mean_last(x):
    return jnp.mean(x, axis=-1, keepdims=True)


def layer_normalise(x):
    average = mean_last(x)
    centred = x - average
    variance = mean_last(centred * centred)
    return centred * lax.rsqrt(variance + EPS)


def transition(middle, cot, expand, half_shrink):
    average = mean_last(middle)
    centred = middle - average
    variance = mean_last(centred * centred)
    inverse = lax.rsqrt(variance + EPS)
    spread = centred * inverse
    before = dot_nn(spread.astype(BF16), expand)
    both = 1.0 + lax.erf(before * 0.7071067811865476)
    hidden = (before * both).astype(BF16)
    result = middle + dot_nn(hidden, half_shrink)
    slope = both + (before * 0.7978845608028654) * jnp.exp2((before * before) * -0.7213475204444817)
    back_hidden = dot_nt(cot.astype(BF16), half_shrink)
    back_before = (back_hidden * slope).astype(BF16)
    back_spread = dot_nt(back_before, expand)
    centre = mean_last(back_spread)
    along = mean_last(back_spread * spread)
    back = cot + inverse * (back_spread - centre - spread * along)
    return result, back


def identity(n):
    rows = lax.broadcasted_iota(jnp.int32, (n, n), 0)
    cols = lax.broadcasted_iota(jnp.int32, (n, n), 1)
    return jnp.where(rows == cols, 1.0, 0.0).astype(BF16)


def attend(x, wq, wk, wv, wg, gate_bias, wo):
    flat = x.reshape(2 * SEQ, 256).astype(F32)
    rows = layer_normalise(flat).astype(BF16)
    query = dot_nn(rows, wq).astype(BF16)
    key = dot_nn(rows, wk).astype(BF16)
    value = dot_nn(rows, wv).astype(BF16)
    gating = jax.nn.sigmoid(dot_nn(rows, wg) + gate_bias)
    head_of = lax.broadcasted_iota(jnp.int32, (SEQ, 256), 1) // HEAD_W
    blended = []
    for n in range(2):
        part = slice(n * SEQ, (n + 1) * SEQ)
        q32 = query[part].astype(F32)
        masked = jnp.concatenate(
            [jnp.where(head_of == h, q32, 0.0).astype(BF16) for h in range(HEADS)], axis=0
        )
        scores = dot_nt(masked, key[part]) * HEAD_W ** (-0.5)
        raised = jnp.exp(scores - jnp.max(scores, axis=-1, keepdims=True))
        totals = jnp.sum(raised, axis=-1, keepdims=True)
        mixed = dot_nn(raised.astype(BF16), value[part]) / totals
        total = jnp.zeros((SEQ, 256), F32)
        for h in range(HEADS):
            total = jnp.where(head_of == h, mixed[h * SEQ : (h + 1) * SEQ], total)
        blended.append(total)
    gated = (gating * jnp.concatenate(blended, axis=0)).astype(BF16)
    return (flat + dot_nn(gated, wo)).astype(BF16)


def kernel(
    a_ref, wq, wk, wv, wg, gate_bias, wo, wleft, wright, w_ref, bias_ref, expand_ref, shrink_ref,
    pf_hbm, ct_hbm,
    upd_ref, out_hbm, gl_ref, gr_ref,
    wide, x_ref, xbuf, ubuf, urecv, half, proj, lsend, rsend, ltbuf, rtbuf, rtf, rt, r2, wf, wbd,
    pf, ct, out, osc, mid, bmsc, bsc, gacc, glsend, glrecv, grsend, grrecv,
    xs, xr, ls, lr, rs, rr, us, ur, gs, gr_sem, hs, hr, mem,
):
    row = lax.axis_index("row")
    col = lax.axis_index("col")
    owner = col // 2
    diagonal = row == owner
    my_source = lax.rem(col, 2) * ROWS + row

    barrier = pltpu.get_barrier_semaphore()

    @pl.loop(1, ROWS)
    def _(off):
        pl.semaphore_signal(barrier, inc=1, device_id=(lax.rem(row + off, ROWS), col), device_id_type=MESH)

    @pl.loop(1, COLS)
    def _(off):
        pl.semaphore_signal(barrier, inc=1, device_id=(row, lax.rem(col + off, COLS)), device_id_type=MESH)

    @pl.loop(0, 2 * ROWS)
    def _(n):
        r, c = lax.rem(n, ROWS), 2 * row + n // ROWS

        @pl.when(jnp.logical_not(jnp.logical_and(r == row, c == col)))
        def _():
            pl.semaphore_signal(barrier, inc=1, device_id=(r, c), device_id_type=MESH)

    load_pf = pltpu.make_async_copy(pf_hbm, pf, mem.at[0])
    load_ct = pltpu.make_async_copy(ct_hbm, ct, mem.at[1])
    load_pf.start()
    load_ct.start()

    eye = identity(128)
    proj[0:32, :] = wleft[...]
    proj[32:64, :] = wright[...]
    half[...] = (shrink_ref[...].astype(F32) * 0.5).astype(BF16)
    for n in range(2):
        lanes = pl.ds(128 * n, 128)
        wide[pl.ds(768 * n, 768), :] = a_ref[:, lanes].astype(F32)
        for r in range(48):
            x_ref[r, :, lanes] = wide[pl.ds(768 * n + r, 16, stride=48), :].astype(BF16)
    wf[...] = w_ref[...].astype(F32)
    wbd[...] = jnp.zeros_like(wbd)
    for e in range(FACTOR):
        block = wf[pl.ds(e, FACTOR, stride=FACTOR), :].astype(BF16)
        for q in range(4):
            wbd[pl.ds(e * 128 + q * 32, 32), pl.ds(q * 128, 128)] = block
    gacc[...] = jnp.zeros_like(gacc)

    pl.semaphore_wait(barrier, ROWS - 1 + COLS - 1 + 2 * ROWS - jnp.where(diagonal, 1, 0))

    def x_copy(t, peer, slot):
        return pltpu.make_async_remote_copy(
            src_ref=x_ref.at[pl.ds(6 * peer + 2 * t, 2)],
            dst_ref=xbuf.at[pl.ds(2 * t, 2), pl.ds(pl.multiple_of(16 * slot, 16), 16)],
            send_sem=xs.at[t, peer],
            recv_sem=xr.at[t, slot],
            device_id=(peer, col),
            device_id_type=MESH,
        )

    @pl.loop(0, STAGES)
    def _(t):
        @pl.loop(1, ROWS)
        def _(off):
            x_copy(t, lax.rem(row + off, ROWS), row).start()

        xbuf[pl.ds(2 * t, 2), pl.ds(pl.multiple_of(16 * row, 16), 16)] = x_ref[pl.ds(6 * row + 2 * t, 2)]

    def l_copy(t, target, source):
        return pltpu.make_async_remote_copy(
            src_ref=lsend.at[t],
            dst_ref=ltbuf.at[t, source],
            send_sem=ls.at[t, target],
            recv_sem=lr.at[t, source],
            device_id=(owner, target),
            device_id_type=MESH,
        )

    def send_left(t):
        @pl.when(jnp.logical_not(diagonal))
        def _():
            l_copy(t, col, my_source).start()

        @pl.when(diagonal)
        def _():
            ltbuf[t, my_source] = lsend[t]

        @pl.loop(1, COLS)
        def _(off):
            l_copy(t, lax.rem(col + off, COLS), my_source).start()

    def r_copy(t, peer, slot):
        return pltpu.make_async_remote_copy(
            src_ref=rsend.at[t],
            dst_ref=rtbuf.at[pl.ds(6 * slot + 2 * t, 2)],
            send_sem=rs.at[t, peer],
            recv_sem=rr.at[t, slot],
            device_id=(peer, col),
            device_id_type=MESH,
        )

    @pl.loop(0, STAGES)
    def _(t):
        @pl.loop(1, ROWS)
        def _(off):
            peer = lax.rem(row + off, ROWS)
            x_copy(t, peer, peer).wait_recv()

        new = attend(
            xbuf[pl.ds(2 * t, 2)], wq[...], wk[...], wv[...], wg[...], gate_bias[...], wo[...]
        )
        ubuf[pl.ds(2 * t, 2)] = new.reshape(2, SEQ, 256)
        factors = dot_nt(proj[...], layer_normalise(new.astype(F32)).astype(BF16))
        left = factors[:32].astype(BF16)
        right = (factors[32:] * (1.0 / SEQ)).astype(BF16)
        for n in range(2):
            lsend[t, n] = left[:, n * SEQ : (n + 1) * SEQ]
            rsend[t, n] = right[:, n * SEQ : (n + 1) * SEQ]

        @pl.loop(1, ROWS)
        def _(off):
            r_copy(t, lax.rem(row + off, ROWS), row).start()

        rtbuf[pl.ds(6 * row + 2 * t, 2)] = rsend[t]

        @pl.when(t == 0)
        def _():
            send_left(0)

    send_left(1)
    send_left(2)

    def u_copy(peer, slot):
        return pltpu.make_async_remote_copy(
            src_ref=ubuf.at[:, pl.ds(pl.multiple_of(16 * peer, 16), 16)],
            dst_ref=urecv.at[pl.ds(6 * slot, 6)],
            send_sem=us.at[peer],
            recv_sem=ur.at[slot],
            device_id=(peer, col),
            device_id_type=MESH,
        )

    @pl.loop(1, ROWS)
    def _(off):
        u_copy(lax.rem(row + off, ROWS), row).start()

    urecv[pl.ds(6 * row, 6)] = ubuf[:, pl.ds(pl.multiple_of(16 * row, 16), 16)]

    @pl.loop(0, STAGES)
    def _(t):
        @pl.loop(1, ROWS)
        def _(off):
            peer = lax.rem(row + off, ROWS)
            r_copy(t, peer, peer).wait_recv()

    for j in range(N_J):
        rtf[pl.ds(j, FACTOR, stride=N_J), :] = rtbuf[j].astype(F32)
    rt[...] = rtf[...].astype(BF16)
    r2[...] = dot_nt(eye, rt[...]).astype(BF16)
    load_pf.wait()
    load_ct.wait()

    def gl_copy(q, target, source):
        return pltpu.make_async_remote_copy(
            src_ref=glsend.at[q, target],
            dst_ref=glrecv.at[q, source],
            send_sem=gs.at[q, target],
            recv_sem=gr_sem.at[q, source],
            device_id=(row, target),
            device_id_type=MESH,
        )

    def store_copy(q):
        part = (slice(None), pl.ds(2 * q, 2))
        return pltpu.make_async_copy(out.at[part], out_hbm.at[part], mem.at[3 + q])

    def gr_copy(peer, slot):
        return pltpu.make_async_remote_copy(
            src_ref=grsend.at[peer],
            dst_ref=grrecv.at[slot],
            send_sem=hs.at[peer],
            recv_sem=hr.at[slot],
            device_id=(peer, col),
            device_id_type=MESH,
        )

    @pl.loop(0, STAGES)
    def _(q):
        @pl.loop(0, 2 * ROWS)
        def _(n):
            @pl.when(jnp.logical_not(jnp.logical_and(diagonal, n == my_source)))
            def _():
                l_copy(q, col, n).wait_recv()

        lt = ltbuf[q].reshape(N_I * FACTOR, SEQ)

        for eb in range(4):
            o = dot_nt(rt[pl.ds(eb * 384, 384), :], lt).astype(BF16)
            for e in range(8):
                for g in range(N_G):
                    osc[pl.ds(g * N_J, N_J), pl.ds(eb * 1024 + e * 128, 128)] = o[
                        e * N_J : (e + 1) * N_J, g * 128 : (g + 1) * 128
                    ]

        mid[...] = dot_nn(osc[...], wbd[...])

        @pl.loop(0, N_G // UNROLL)
        def _(gs_):
            for gu in range(UNROLL):
                g = gs_ * UNROLL + gu
                rows = pl.ds(pl.multiple_of(g * N_J, N_J), N_J)
                block = mid[rows, :]
                x = jnp.concatenate([block[:, n * 128 : (n + 1) * 128] for n in range(4)], axis=0)
                part = (pl.ds(g * 2, 2), pl.ds(q * 2, 2))
                cot = ct[part].reshape(4 * N_J, PAIR_W)
                x = pf[part].reshape(4 * N_J, PAIR_W) + x + bias_ref[...]
                result, back = transition(x, cot, expand_ref[...], half[...])
                out[part] = result.reshape(2, 2, N_J, PAIR_W)
                back = back.astype(BF16)
                for n in range(4):
                    bmsc[rows, pl.ds(n * 128, 128)] = back[n * N_J : (n + 1) * N_J, :]

        store_copy(q).start()

        for eb in range(4):
            part = pl.ds(eb * 384, 384)
            b = dot_nt(bmsc[...], wbd[pl.ds(eb * 1024, 1024), :]).astype(BF16)
            for e in range(8):
                for g in range(N_G):
                    bsc[pl.ds(eb * 384 + e * N_J, N_J), pl.ds(g * 128, 128)] = b[
                        g * N_J : (g + 1) * N_J, e * 128 : (e + 1) * 128
                    ]
            gacc[part, :] += dot_nn(bsc[part, :], lt)

        @pl.when(q == STAGES - 1)
        def _():
            by_residue = jnp.concatenate(
                [gacc[pl.ds(j, FACTOR, stride=N_J), :] for j in range(N_J)], axis=0
            )
            grt = dot_nt(eye, (by_residue * (1.0 / SEQ)).astype(BF16)).astype(BF16)
            for d in range(ROWS):
                grsend[d] = grt[16 * d : 16 * d + 16]

            @pl.loop(1, ROWS)
            def _(off):
                gr_copy(lax.rem(row + off, ROWS), row).start()

        gl = dot_nn(r2[...], bsc[...])
        for d in range(COLS):
            part = gl[8 * d : 8 * d + 8]
            glsend[q, d] = jnp.concatenate([part[:, :512], part[:, 512:]], axis=0).astype(BF16)

        @pl.loop(1, COLS)
        def _(off):
            gl_copy(q, lax.rem(col + off, COLS), col).start()

    @pl.loop(1, ROWS)
    def _(off):
        peer = lax.rem(row + off, ROWS)
        u_copy(peer, peer).wait_recv()

    for n in range(2):
        lanes = pl.ds(128 * n, 128)
        for r in range(48):
            wide[pl.ds(768 * n + r, 16, stride=48), :] = urecv[r, :, lanes].astype(F32)
        upd_ref[:, lanes] = wide[pl.ds(768 * n, 768), :].astype(BF16)

    sums = []
    for q in range(STAGES):
        glrecv[q, col] = glsend[q, col]

        @pl.loop(1, COLS)
        def _(off):
            source = lax.rem(col + off, COLS)
            gl_copy(q, source, source).wait_recv()

        total = glrecv[q, 0].astype(F32)
        for n in range(1, COLS):
            total = total + glrecv[q, n].astype(F32)
        sums.append(total)
    for half_of in range(2):
        pieces = [
            sums[q][8 * half_of : 8 * half_of + 8, 64 * n : 64 * n + 64] for n in range(8) for q in range(STAGES)
        ]
        gl_ref[:, pl.ds(1536 * half_of, 1536)] = jnp.concatenate(pieces, axis=1)

    grrecv[row] = grsend[row]

    @pl.loop(1, ROWS)
    def _(off):
        peer = lax.rem(row + off, ROWS)
        gr_copy(peer, peer).wait_recv()

    total = jnp.zeros((16, N_J * FACTOR), F32)
    for s in range(ROWS):
        total = total + grrecv[s].astype(F32)
    gr_ref[...] = total

    @pl.loop(1, ROWS)
    def _(off):
        peer = lax.rem(row + off, ROWS)
        u_copy(peer, row).wait_send()
        gr_copy(peer, row).wait_send()

    @pl.loop(0, STAGES)
    def _(t):
        store_copy(t).wait()

        @pl.loop(1, ROWS)
        def _(off):
            peer = lax.rem(row + off, ROWS)
            x_copy(t, peer, row).wait_send()
            r_copy(t, peer, row).wait_send()

        @pl.when(jnp.logical_not(diagonal))
        def _():
            l_copy(t, col, my_source).wait_send()

        @pl.loop(1, COLS)
        def _(off):
            target = lax.rem(col + off, COLS)
            l_copy(t, target, my_source).wait_send()
            gl_copy(t, target, col).wait_send()


def local(
    alignment, pair_features, query_weight, key_weight, value_projection, gate_projection,
    gate_bias, output_projection, left_projection, right_projection, outer_weight, outer_bias,
    expand_weight, shrink_weight, cotangent,
):
    vmem = pl.BlockSpec(memory_space=pltpu.VMEM)
    hbm = pl.BlockSpec(memory_space=pl.ANY)
    dma = pltpu.SemaphoreType.DMA
    upd, out, gl, gr = pl.pallas_call(
        kernel,
        in_specs=[vmem] * 13 + [hbm] * 2,
        out_specs=[vmem, hbm, vmem, vmem],
        out_shape=[
            jax.ShapeDtypeStruct((16 * 48, 256), BF16),
            jax.ShapeDtypeStruct((16, 6, N_J, PAIR_W), F32),
            jax.ShapeDtypeStruct((8, 3072), F32),
            jax.ShapeDtypeStruct((16, N_J * FACTOR), F32),
        ],
        scratch_shapes=[
            pltpu.VMEM((2 * 16 * 48, 128), F32),
            pltpu.VMEM((48, 16, 256), BF16),
            pltpu.VMEM((6, SEQ, 256), BF16),
            pltpu.VMEM((6, SEQ, 256), BF16),
            pltpu.VMEM((48, 16, 256), BF16),
            pltpu.VMEM((512, PAIR_W), BF16),
            pltpu.VMEM((64, 256), BF16),
            pltpu.VMEM((STAGES, 2, FACTOR, SEQ), BF16),
            pltpu.VMEM((STAGES, 2, FACTOR, SEQ), BF16),
            pltpu.VMEM((STAGES, 16, 2, FACTOR, SEQ), BF16),
            pltpu.VMEM((N_J, FACTOR, SEQ), BF16),
            pltpu.VMEM((FACTOR * N_J, SEQ), F32),
            pltpu.VMEM((FACTOR * N_J, SEQ), BF16),
            pltpu.VMEM((SEQ, FACTOR * N_J), BF16),
            pltpu.VMEM((FACTOR * FACTOR, PAIR_W), F32),
            pltpu.VMEM((4096, 512), BF16),
            pltpu.VMEM((16, 6, N_J, PAIR_W), F32),
            pltpu.VMEM((16, 6, N_J, PAIR_W), F32),
            pltpu.VMEM((16, 6, N_J, PAIR_W), F32),
            pltpu.VMEM((N_G * N_J, 4096), BF16),
            pltpu.VMEM((N_G * N_J, 512), F32),
            pltpu.VMEM((N_G * N_J, 512), BF16),
            pltpu.VMEM((FACTOR * N_J, 1024), BF16),
            pltpu.VMEM((FACTOR * N_J, SEQ), F32),
            pltpu.VMEM((STAGES, COLS, 16, 512), BF16),
            pltpu.VMEM((STAGES, COLS, 16, 512), BF16),
            pltpu.VMEM((ROWS, 16, N_J * FACTOR), BF16),
            pltpu.VMEM((ROWS, 16, N_J * FACTOR), BF16),
            dma((STAGES, ROWS)), dma((STAGES, ROWS)),
            dma((STAGES, COLS)), dma((STAGES, COLS)),
            dma((STAGES, ROWS)), dma((STAGES, ROWS)),
            dma((ROWS,)), dma((ROWS,)),
            dma((STAGES, COLS)), dma((STAGES, COLS)),
            dma((ROWS,)), dma((ROWS,)),
            dma((6,)),
        ],
        compiler_params=pltpu.CompilerParams(
            collective_id=0, has_side_effects=True, vmem_limit_bytes=60 * 1024 * 1024
        ),
        name="block",
    )(
        alignment.reshape(16 * 48, 256), query_weight, key_weight, value_projection, gate_projection,
        gate_bias.reshape(1, -1), output_projection, left_projection.T, right_projection.T,
        outer_weight, outer_bias.reshape(1, -1), expand_weight, shrink_weight,
        pair_features.reshape(16, 6, N_J, PAIR_W), cotangent.reshape(16, 6, N_J, PAIR_W),
    )
    return upd.reshape(16, 48, 256), out.reshape(96, N_J, PAIR_W), gl, gr


def solution(mesh):
    return jax.shard_map(
        local,
        mesh=mesh,
        in_specs=(P("row", "col", None), P("row", "col", None)) + (P(),) * 12 + (P("row", "col", None),),
        out_specs=(P("row", "col", None), P("row", "col", None), P("col", "row"), P("row", "col")),
        check_vma=False,
    )
```

```python
import jax
import jax.numpy as jnp
from jax import lax
from jax.experimental import pallas as pl
from jax.experimental.pallas import tpu as pltpu
from jax.sharding import PartitionSpec as P

HEADS = 8
HEAD_W = 32
FACTOR = 32
PAIR_W = 128
EPS = 1e-05
F32 = jnp.float32
BF16 = jnp.bfloat16
MESH = pl.DeviceIdType.MESH
UNROLL = 4

ROWS = 8
COLS = 16
SEQ = 128
STAGES = 3
N_J = 48
N_I = 32
N_G = N_I // 4


def dot_nn(a, b):
    return jnp.dot(a, b, preferred_element_type=F32)


def dot_nt(a, b):
    return lax.dot_general(a, b, (((1,), (1,)), ((), ())), preferred_element_type=F32)


def mean_last(x):
    return jnp.mean(x, axis=-1, keepdims=True)


def layer_normalise(x):
    average = mean_last(x)
    centred = x - average
    variance = mean_last(centred * centred)
    return centred * lax.rsqrt(variance + EPS)


def transition(middle, cot, expand, half_shrink):
    average = mean_last(middle)
    centred = middle - average
    variance = mean_last(centred * centred)
    inverse = lax.rsqrt(variance + EPS)
    spread = centred * inverse
    before = dot_nn(spread.astype(BF16), expand)
    both = 1.0 + lax.erf(before * 0.7071067811865476)
    hidden = (before * both).astype(BF16)
    result = middle + dot_nn(hidden, half_shrink)
    slope = both + (before * 0.7978845608028654) * jnp.exp2((before * before) * -0.7213475204444817)
    back_hidden = dot_nt(cot.astype(BF16), half_shrink)
    back_before = (back_hidden * slope).astype(BF16)
    back_spread = dot_nt(back_before, expand)
    centre = mean_last(back_spread)
    along = mean_last(back_spread * spread)
    back = cot + inverse * (back_spread - centre - spread * along)
    return result, back


def identity(n):
    rows = lax.broadcasted_iota(jnp.int32, (n, n), 0)
    cols = lax.broadcasted_iota(jnp.int32, (n, n), 1)
    return jnp.where(rows == cols, 1.0, 0.0).astype(BF16)


def attend(x, wq, wk, wv, wg, gate_bias, wo):
    flat = x.reshape(2 * SEQ, 256).astype(F32)
    rows = layer_normalise(flat).astype(BF16)
    query = dot_nn(rows, wq).astype(BF16)
    key = dot_nn(rows, wk).astype(BF16)
    value = dot_nn(rows, wv).astype(BF16)
    gating = jax.nn.sigmoid(dot_nn(rows, wg) + gate_bias)
    head_of = lax.broadcasted_iota(jnp.int32, (SEQ, 256), 1) // HEAD_W
    blended = []
    for n in range(2):
        part = slice(n * SEQ, (n + 1) * SEQ)
        q32 = query[part].astype(F32)
        masked = jnp.concatenate(
            [jnp.where(head_of == h, q32, 0.0).astype(BF16) for h in range(HEADS)], axis=0
        )
        scores = dot_nt(masked, key[part]) * HEAD_W ** (-0.5)
        raised = jnp.exp(scores - jnp.max(scores, axis=-1, keepdims=True))
        totals = jnp.sum(raised, axis=-1, keepdims=True)
        mixed = dot_nn(raised.astype(BF16), value[part]) / totals
        total = jnp.zeros((SEQ, 256), F32)
        for h in range(HEADS):
            total = jnp.where(head_of == h, mixed[h * SEQ : (h + 1) * SEQ], total)
        blended.append(total)
    gated = (gating * jnp.concatenate(blended, axis=0)).astype(BF16)
    return (flat + dot_nn(gated, wo)).astype(BF16)


def kernel(
    a_ref, wq, wk, wv, wg, gate_bias, wo, wleft, wright, w_ref, bias_ref, expand_ref, shrink_ref,
    pf_hbm, ct_hbm,
    upd_ref, out_hbm, gl_ref, gr_ref,
    wide, x_ref, xbuf, ubuf, urecv, half, proj, lsend, rsend, ltbuf, rtbuf, rtf, rt, r2, wf, wbd,
    pf, ct, out, osc, mid, bmsc, bsc, gacc, glsend, glrecv, grsend, grrecv,
    xs, xr, ls, lr, ms, mr, rs, rr, us, ur, gs, gr_sem, hs, hr, mem,
):
    row = lax.axis_index("row")
    col = lax.axis_index("col")
    across, along = col // 4, lax.rem(col, 4)
    owner = col // 2
    diagonal = row == owner
    half_of_col = lax.rem(col, 2)
    relay = along // 2 == lax.rem(row, 2)

    barrier = pltpu.get_barrier_semaphore()

    @pl.loop(1, ROWS)
    def _(off):
        pl.semaphore_signal(barrier, inc=1, device_id=(lax.rem(row + off, ROWS), col), device_id_type=MESH)

    @pl.loop(1, COLS)
    def _(off):
        pl.semaphore_signal(barrier, inc=1, device_id=(row, lax.rem(col + off, COLS)), device_id_type=MESH)

    @pl.when(relay)
    def _():
        @pl.loop(0, ROWS)
        def _(r):
            @pl.when(jnp.logical_not(jnp.logical_and(diagonal, r == row)))
            def _():
                pl.semaphore_signal(
                    barrier, inc=1, device_id=(r, (row // 2) * 4 + along), device_id_type=MESH
                )

    load_pf = pltpu.make_async_copy(pf_hbm, pf, mem.at[0])
    load_ct = pltpu.make_async_copy(ct_hbm, ct, mem.at[1])
    load_pf.start()
    load_ct.start()

    eye = identity(128)
    proj[0:32, :] = wleft[...]
    proj[32:64, :] = wright[...]
    half[...] = (shrink_ref[...].astype(F32) * 0.5).astype(BF16)
    for n in range(2):
        lanes = pl.ds(128 * n, 128)
        wide[pl.ds(768 * n, 768), :] = a_ref[:, lanes].astype(F32)
        for r in range(48):
            x_ref[r, :, lanes] = wide[pl.ds(768 * n + r, 16, stride=48), :].astype(BF16)
    wf[...] = w_ref[...].astype(F32)
    wbd[...] = jnp.zeros_like(wbd)
    for e in range(FACTOR):
        block = wf[pl.ds(e, FACTOR, stride=FACTOR), :].astype(BF16)
        for q in range(4):
            wbd[pl.ds(e * 128 + q * 32, 32), pl.ds(q * 128, 128)] = block
    gacc[...] = jnp.zeros_like(gacc)

    pl.semaphore_wait(barrier, ROWS - 1 + COLS - 1 + 4 - jnp.where(diagonal, 1, 0))

    def x_copy(t, peer, slot):
        return pltpu.make_async_remote_copy(
            src_ref=x_ref.at[pl.ds(6 * peer + 2 * t, 2)],
            dst_ref=xbuf.at[pl.ds(2 * t, 2), pl.ds(pl.multiple_of(16 * slot, 16), 16)],
            send_sem=xs.at[t, peer],
            recv_sem=xr.at[t, slot],
            device_id=(peer, col),
            device_id_type=MESH,
        )

    @pl.loop(0, STAGES)
    def _(t):
        @pl.loop(1, ROWS)
        def _(off):
            x_copy(t, lax.rem(row + off, ROWS), row).start()

        xbuf[pl.ds(2 * t, 2), pl.ds(pl.multiple_of(16 * row, 16), 16)] = x_ref[pl.ds(6 * row + 2 * t, 2)]

    def l_copy(t, x, source):
        return pltpu.make_async_remote_copy(
            src_ref=lsend.at[t],
            dst_ref=ltbuf.at[t, half_of_col * ROWS + source],
            send_sem=ls.at[t, x],
            recv_sem=lr.at[t, source],
            device_id=(owner, x * 4 + along),
            device_id_type=MESH,
        )

    def pass_copy(t, half_index, z):
        part = ltbuf.at[t, pl.ds(pl.multiple_of(half_index * ROWS, ROWS), ROWS)]
        return pltpu.make_async_remote_copy(
            src_ref=part,
            dst_ref=part,
            send_sem=ms.at[t, z],
            recv_sem=mr.at[t, half_index],
            device_id=(row, across * 4 + z),
            device_id_type=MESH,
        )

    def send_left(t):
        @pl.when(jnp.logical_not(diagonal))
        def _():
            l_copy(t, across, row).start()

        @pl.when(diagonal)
        def _():
            ltbuf[t, half_of_col * ROWS + row] = lsend[t]

        @pl.loop(1, 4)
        def _(off):
            l_copy(t, lax.rem(across + off, 4), row).start()

    def pass_left(t):
        @pl.when(relay)
        def _():
            @pl.loop(0, ROWS)
            def _(r):
                @pl.when(jnp.logical_not(jnp.logical_and(diagonal, r == row)))
                def _():
                    l_copy(t, across, r).wait_recv()

            @pl.loop(1, 4)
            def _(off):
                pass_copy(t, half_of_col, lax.rem(along + off, 4)).start()

    def r_copy(t, peer, slot):
        return pltpu.make_async_remote_copy(
            src_ref=rsend.at[t],
            dst_ref=rtbuf.at[pl.ds(6 * slot + 2 * t, 2)],
            send_sem=rs.at[t, peer],
            recv_sem=rr.at[t, slot],
            device_id=(peer, col),
            device_id_type=MESH,
        )

    @pl.loop(0, STAGES)
    def _(t):
        @pl.loop(1, ROWS)
        def _(off):
            peer = lax.rem(row + off, ROWS)
            x_copy(t, peer, peer).wait_recv()

        new = attend(
            xbuf[pl.ds(2 * t, 2)], wq[...], wk[...], wv[...], wg[...], gate_bias[...], wo[...]
        )
        ubuf[pl.ds(2 * t, 2)] = new.reshape(2, SEQ, 256)
        factors = dot_nt(proj[...], layer_normalise(new.astype(F32)).astype(BF16))
        left = factors[:32].astype(BF16)
        right = (factors[32:] * (1.0 / SEQ)).astype(BF16)
        for n in range(2):
            lsend[t, n] = left[:, n * SEQ : (n + 1) * SEQ]
            rsend[t, n] = right[:, n * SEQ : (n + 1) * SEQ]

        @pl.loop(1, ROWS)
        def _(off):
            r_copy(t, lax.rem(row + off, ROWS), row).start()

        rtbuf[pl.ds(6 * row + 2 * t, 2)] = rsend[t]

        send_left(t)

        @pl.when(t > 0)
        def _():
            pass_left(t - 1)

    def u_copy(peer, slot):
        return pltpu.make_async_remote_copy(
            src_ref=ubuf.at[:, pl.ds(pl.multiple_of(16 * peer, 16), 16)],
            dst_ref=urecv.at[pl.ds(6 * slot, 6)],
            send_sem=us.at[peer],
            recv_sem=ur.at[slot],
            device_id=(peer, col),
            device_id_type=MESH,
        )

    @pl.loop(1, ROWS)
    def _(off):
        u_copy(lax.rem(row + off, ROWS), row).start()

    urecv[pl.ds(6 * row, 6)] = ubuf[:, pl.ds(pl.multiple_of(16 * row, 16), 16)]

    @pl.loop(0, STAGES)
    def _(t):
        @pl.loop(1, ROWS)
        def _(off):
            peer = lax.rem(row + off, ROWS)
            r_copy(t, peer, peer).wait_recv()

    pass_left(STAGES - 1)

    for j in range(N_J):
        rtf[pl.ds(j, FACTOR, stride=N_J), :] = rtbuf[j].astype(F32)
    rt[...] = rtf[...].astype(BF16)
    r2[...] = dot_nt(eye, rt[...]).astype(BF16)
    load_pf.wait()
    load_ct.wait()

    def gl_copy(q, target, source):
        return pltpu.make_async_remote_copy(
            src_ref=glsend.at[q, target],
            dst_ref=glrecv.at[q, source],
            send_sem=gs.at[q, target],
            recv_sem=gr_sem.at[q, source],
            device_id=(row, target),
            device_id_type=MESH,
        )

    def store_copy(q):
        part = (slice(None), pl.ds(2 * q, 2))
        return pltpu.make_async_copy(out.at[part], out_hbm.at[part], mem.at[3 + q])

    def gr_copy(peer, slot):
        return pltpu.make_async_remote_copy(
            src_ref=grsend.at[peer],
            dst_ref=grrecv.at[slot],
            send_sem=hs.at[peer],
            recv_sem=hr.at[slot],
            device_id=(peer, col),
            device_id_type=MESH,
        )

    @pl.loop(0, STAGES)
    def _(q):
        for n in range(2):
            @pl.when(jnp.logical_not(jnp.logical_and(relay, half_of_col == n)))
            def _():
                pass_copy(q, n, along).wait_recv()

        lt = ltbuf[q].reshape(N_I * FACTOR, SEQ)

        for eb in range(4):
            o = dot_nt(rt[pl.ds(eb * 384, 384), :], lt).astype(BF16)
            for e in range(8):
                for g in range(N_G):
                    osc[pl.ds(g * N_J, N_J), pl.ds(eb * 1024 + e * 128, 128)] = o[
                        e * N_J : (e + 1) * N_J, g * 128 : (g + 1) * 128
                    ]

        mid[...] = dot_nn(osc[...], wbd[...])

        @pl.loop(0, N_G // UNROLL)
        def _(gs_):
            for gu in range(UNROLL):
                g = gs_ * UNROLL + gu
                rows = pl.ds(pl.multiple_of(g * N_J, N_J), N_J)
                block = mid[rows, :]
                x = jnp.concatenate([block[:, n * 128 : (n + 1) * 128] for n in range(4)], axis=0)
                part = (pl.ds(g * 2, 2), pl.ds(q * 2, 2))
                cot = ct[part].reshape(4 * N_J, PAIR_W)
                x = pf[part].reshape(4 * N_J, PAIR_W) + x + bias_ref[...]
                result, back = transition(x, cot, expand_ref[...], half[...])
                out[part] = result.reshape(2, 2, N_J, PAIR_W)
                back = back.astype(BF16)
                for n in range(4):
                    bmsc[rows, pl.ds(n * 128, 128)] = back[n * N_J : (n + 1) * N_J, :]

        store_copy(q).start()

        for eb in range(4):
            part = pl.ds(eb * 384, 384)
            b = dot_nt(bmsc[...], wbd[pl.ds(eb * 1024, 1024), :]).astype(BF16)
            for e in range(8):
                for g in range(N_G):
                    bsc[pl.ds(eb * 384 + e * N_J, N_J), pl.ds(g * 128, 128)] = b[
                        g * N_J : (g + 1) * N_J, e * 128 : (e + 1) * 128
                    ]
            gacc[part, :] += dot_nn(bsc[part, :], lt)

        @pl.when(q == STAGES - 1)
        def _():
            by_residue = jnp.concatenate(
                [gacc[pl.ds(j, FACTOR, stride=N_J), :] for j in range(N_J)], axis=0
            )
            grt = dot_nt(eye, (by_residue * (1.0 / SEQ)).astype(BF16)).astype(BF16)
            for d in range(ROWS):
                grsend[d] = grt[16 * d : 16 * d + 16]

            @pl.loop(1, ROWS)
            def _(off):
                gr_copy(lax.rem(row + off, ROWS), row).start()

        gl = dot_nn(r2[...], bsc[...])
        for d in range(COLS):
            part = gl[8 * d : 8 * d + 8]
            glsend[q, d] = jnp.concatenate([part[:, :512], part[:, 512:]], axis=0).astype(BF16)

        @pl.loop(1, COLS)
        def _(off):
            gl_copy(q, lax.rem(col + off, COLS), col).start()

    @pl.loop(1, ROWS)
    def _(off):
        peer = lax.rem(row + off, ROWS)
        u_copy(peer, peer).wait_recv()

    for n in range(2):
        lanes = pl.ds(128 * n, 128)
        for r in range(48):
            wide[pl.ds(768 * n + r, 16, stride=48), :] = urecv[r, :, lanes].astype(F32)
        upd_ref[:, lanes] = wide[pl.ds(768 * n, 768), :].astype(BF16)

    sums = []
    for q in range(STAGES):
        glrecv[q, col] = glsend[q, col]

        @pl.loop(1, COLS)
        def _(off):
            source = lax.rem(col + off, COLS)
            gl_copy(q, source, source).wait_recv()

        total = glrecv[q, 0].astype(F32)
        for n in range(1, COLS):
            total = total + glrecv[q, n].astype(F32)
        sums.append(total)
    for half_of in range(2):
        pieces = [
            sums[q][8 * half_of : 8 * half_of + 8, 64 * n : 64 * n + 64] for n in range(8) for q in range(STAGES)
        ]
        gl_ref[:, pl.ds(1536 * half_of, 1536)] = jnp.concatenate(pieces, axis=1)

    grrecv[row] = grsend[row]

    @pl.loop(1, ROWS)
    def _(off):
        peer = lax.rem(row + off, ROWS)
        gr_copy(peer, peer).wait_recv()

    total = jnp.zeros((16, N_J * FACTOR), F32)
    for s in range(ROWS):
        total = total + grrecv[s].astype(F32)
    gr_ref[...] = total

    @pl.loop(1, ROWS)
    def _(off):
        peer = lax.rem(row + off, ROWS)
        u_copy(peer, row).wait_send()
        gr_copy(peer, row).wait_send()

    @pl.loop(0, STAGES)
    def _(t):
        store_copy(t).wait()

        @pl.loop(1, ROWS)
        def _(off):
            peer = lax.rem(row + off, ROWS)
            x_copy(t, peer, row).wait_send()
            r_copy(t, peer, row).wait_send()

        @pl.when(jnp.logical_not(diagonal))
        def _():
            l_copy(t, across, row).wait_send()

        @pl.loop(1, 4)
        def _(off):
            l_copy(t, lax.rem(across + off, 4), row).wait_send()

            @pl.when(relay)
            def _():
                pass_copy(t, half_of_col, lax.rem(along + off, 4)).wait_send()

        @pl.loop(1, COLS)
        def _(off):
            gl_copy(t, lax.rem(col + off, COLS), col).wait_send()


def hand_over(out_in, upd_in, gl_in, gr_in, out_to, upd_to, gl_to, gr_to, out_v, upd_v, gl_v, gr_v, sems):
    jobs = []
    for n in range(4):
        part = pl.ds(4 * n, 4)
        jobs.append((out_in.at[part], out_v.at[part], out_to.at[part]))
    jobs += [(upd_in, upd_v, upd_to), (gl_in, gl_v, gl_to), (gr_in, gr_v, gr_to)]
    first = [pltpu.make_async_copy(a, b, sems.at[0, n]) for n, (a, b, c) in enumerate(jobs)]
    second = [pltpu.make_async_copy(b, c, sems.at[1, n]) for n, (a, b, c) in enumerate(jobs)]
    for copy in first:
        copy.start()
    for a, b in zip(first, second):
        a.wait()
        b.start()
    for copy in second:
        copy.wait()


def local(
    alignment, pair_features, query_weight, key_weight, value_projection, gate_projection,
    gate_bias, output_projection, left_projection, right_projection, outer_weight, outer_bias,
    expand_weight, shrink_weight, cotangent,
):
    vmem = pl.BlockSpec(memory_space=pltpu.VMEM)
    hbm = pl.BlockSpec(memory_space=pl.ANY)
    dma = pltpu.SemaphoreType.DMA
    upd, out, gl, gr = pl.pallas_call(
        kernel,
        in_specs=[vmem] * 13 + [hbm] * 2,
        out_specs=[vmem, hbm, vmem, vmem],
        out_shape=[
            jax.ShapeDtypeStruct((16 * 48, 256), BF16),
            jax.ShapeDtypeStruct((16, 6, N_J, PAIR_W), F32),
            jax.ShapeDtypeStruct((8, 3072), F32),
            jax.ShapeDtypeStruct((16, N_J * FACTOR), F32),
        ],
        scratch_shapes=[
            pltpu.VMEM((2 * 16 * 48, 128), F32),
            pltpu.VMEM((48, 16, 256), BF16),
            pltpu.VMEM((6, SEQ, 256), BF16),
            pltpu.VMEM((6, SEQ, 256), BF16),
            pltpu.VMEM((48, 16, 256), BF16),
            pltpu.VMEM((512, PAIR_W), BF16),
            pltpu.VMEM((64, 256), BF16),
            pltpu.VMEM((STAGES, 2, FACTOR, SEQ), BF16),
            pltpu.VMEM((STAGES, 2, FACTOR, SEQ), BF16),
            pltpu.VMEM((STAGES, 16, 2, FACTOR, SEQ), BF16),
            pltpu.VMEM((N_J, FACTOR, SEQ), BF16),
            pltpu.VMEM((FACTOR * N_J, SEQ), F32),
            pltpu.VMEM((FACTOR * N_J, SEQ), BF16),
            pltpu.VMEM((SEQ, FACTOR * N_J), BF16),
            pltpu.VMEM((FACTOR * FACTOR, PAIR_W), F32),
            pltpu.VMEM((4096, 512), BF16),
            pltpu.VMEM((16, 6, N_J, PAIR_W), F32),
            pltpu.VMEM((16, 6, N_J, PAIR_W), F32),
            pltpu.VMEM((16, 6, N_J, PAIR_W), F32),
            pltpu.VMEM((N_G * N_J, 4096), BF16),
            pltpu.VMEM((N_G * N_J, 512), F32),
            pltpu.VMEM((N_G * N_J, 512), BF16),
            pltpu.VMEM((FACTOR * N_J, 1024), BF16),
            pltpu.VMEM((FACTOR * N_J, SEQ), F32),
            pltpu.VMEM((STAGES, COLS, 16, 512), BF16),
            pltpu.VMEM((STAGES, COLS, 16, 512), BF16),
            pltpu.VMEM((ROWS, 16, N_J * FACTOR), BF16),
            pltpu.VMEM((ROWS, 16, N_J * FACTOR), BF16),
            dma((STAGES, ROWS)), dma((STAGES, ROWS)),
            dma((STAGES, 4)), dma((STAGES, ROWS)),
            dma((STAGES, 4)), dma((STAGES, 2)),
            dma((STAGES, ROWS)), dma((STAGES, ROWS)),
            dma((ROWS,)), dma((ROWS,)),
            dma((STAGES, COLS)), dma((STAGES, COLS)),
            dma((ROWS,)), dma((ROWS,)),
            dma((6,)),
        ],
        compiler_params=pltpu.CompilerParams(
            collective_id=0, has_side_effects=True, vmem_limit_bytes=60 * 1024 * 1024
        ),
        name="block",
    )(
        alignment.reshape(16 * 48, 256), query_weight, key_weight, value_projection, gate_projection,
        gate_bias.reshape(1, -1), output_projection, left_projection.T, right_projection.T,
        outer_weight, outer_bias.reshape(1, -1), expand_weight, shrink_weight,
        pair_features.reshape(16, 6, N_J, PAIR_W), cotangent.reshape(16, 6, N_J, PAIR_W),
    )
    results = (out, upd, gl, gr)
    out, upd, gl, gr = pl.pallas_call(
        hand_over,
        in_specs=[hbm] * 4,
        out_specs=[hbm] * 4,
        out_shape=[jax.ShapeDtypeStruct(a.shape, a.dtype) for a in results],
        scratch_shapes=[pltpu.VMEM(a.shape, a.dtype) for a in results] + [dma((2, 7))],
        name="hand_over",
    )(*results)
    return upd.reshape(16, 48, 256), out.reshape(96, N_J, PAIR_W), gl, gr


def solution(mesh):
    return jax.shard_map(
        local,
        mesh=mesh,
        in_specs=(P("row", "col", None), P("row", "col", None)) + (P(),) * 12 + (P("row", "col", None),),
        out_specs=(P("row", "col", None), P("row", "col", None), P("col", "row"), P("row", "col")),
        check_vma=False,
    )
```

```python
import jax
import jax.numpy as jnp
from jax import lax
from jax.experimental import pallas as pl
from jax.experimental.pallas import tpu as pltpu
from jax.sharding import PartitionSpec as P

HEADS = 8
HEAD_W = 32
FACTOR = 32
PAIR_W = 128
EPS = 1e-05
F32 = jnp.float32
BF16 = jnp.bfloat16
MESH = pl.DeviceIdType.MESH
UNROLL = 4

ROWS = 8
COLS = 16
SEQ = 128
STAGES = 3
N_J = 48
N_I = 32
N_G = N_I // 4


def dot_nn(a, b):
    return jnp.dot(a, b, preferred_element_type=F32)


def dot_nt(a, b):
    return lax.dot_general(a, b, (((1,), (1,)), ((), ())), preferred_element_type=F32)


def mean_last(x):
    return jnp.mean(x, axis=-1, keepdims=True)


def layer_normalise(x):
    average = mean_last(x)
    centred = x - average
    variance = mean_last(centred * centred)
    return centred * lax.rsqrt(variance + EPS)


def transition(middle, cot, expand, half_shrink):
    average = mean_last(middle)
    centred = middle - average
    variance = mean_last(centred * centred)
    inverse = lax.rsqrt(variance + EPS)
    spread = centred * inverse
    before = dot_nn(spread.astype(BF16), expand).astype(BF16)
    both = 1.0 + lax.erf(before * BF16(0.7071067811865476))
    hidden = before * both
    result = middle + dot_nn(hidden, half_shrink)
    slope = both + (before * BF16(0.7978845608028654)) * jnp.exp2((before * before) * BF16(-0.7213475204444817))
    back_hidden = dot_nt(cot.astype(BF16), half_shrink).astype(BF16)
    back_before = back_hidden * slope
    back_spread = dot_nt(back_before, expand)
    centre = mean_last(back_spread)
    along = mean_last(back_spread * spread)
    back = cot + inverse * (back_spread - centre - spread * along)
    return result, back


def identity(n):
    rows = lax.broadcasted_iota(jnp.int32, (n, n), 0)
    cols = lax.broadcasted_iota(jnp.int32, (n, n), 1)
    return jnp.where(rows == cols, 1.0, 0.0).astype(BF16)


def attend(x, wq, wk, wv, wg, gate_bias, wo):
    flat = x.reshape(2 * SEQ, 256).astype(F32)
    rows = layer_normalise(flat).astype(BF16)
    query = dot_nn(rows, wq).astype(BF16)
    key = dot_nn(rows, wk).astype(BF16)
    value = dot_nn(rows, wv).astype(BF16)
    gating = jax.nn.sigmoid(dot_nn(rows, wg) + gate_bias)
    head_of = lax.broadcasted_iota(jnp.int32, (SEQ, 256), 1) // HEAD_W
    blended = []
    for n in range(2):
        part = slice(n * SEQ, (n + 1) * SEQ)
        q32 = query[part].astype(F32)
        masked = jnp.concatenate(
            [jnp.where(head_of == h, q32, 0.0).astype(BF16) for h in range(HEADS)], axis=0
        )
        scores = dot_nt(masked, key[part]) * HEAD_W ** (-0.5)
        raised = jnp.exp(scores - jnp.max(scores, axis=-1, keepdims=True))
        totals = jnp.sum(raised, axis=-1, keepdims=True)
        mixed = dot_nn(raised.astype(BF16), value[part]) / totals
        total = jnp.zeros((SEQ, 256), F32)
        for h in range(HEADS):
            total = jnp.where(head_of == h, mixed[h * SEQ : (h + 1) * SEQ], total)
        blended.append(total)
    gated = (gating * jnp.concatenate(blended, axis=0)).astype(BF16)
    return (flat + dot_nn(gated, wo)).astype(BF16)


def kernel(
    a_ref, wq, wk, wv, wg, gate_bias, wo, wleft, wright, w_ref, bias_ref, expand_ref, shrink_ref,
    pf_hbm, ct_hbm,
    upd_ref, out_hbm, gl_ref, gr_ref,
    wide, x_ref, xbuf, ubuf, urecv, half, proj, lsend, rsend, ltbuf, rtbuf, rtf, rt, r2, wf, wbd,
    pf, ct, out, osc, mid, bmsc, bsc, gacc, glsend, glrecv, grsend, grrecv,
    xs, xr, ls, lr, ms, mr, rs, rr, us, ur, gs, gr_sem, hs, hr, mem,
):
    row = lax.axis_index("row")
    col = lax.axis_index("col")
    across, along = col // 4, lax.rem(col, 4)
    owner = col // 2
    diagonal = row == owner
    half_of_col = lax.rem(col, 2)
    relay = along // 2 == lax.rem(row, 2)

    barrier = pltpu.get_barrier_semaphore()

    @pl.loop(1, ROWS)
    def _(off):
        pl.semaphore_signal(barrier, inc=1, device_id=(lax.rem(row + off, ROWS), col), device_id_type=MESH)

    @pl.loop(1, COLS)
    def _(off):
        pl.semaphore_signal(barrier, inc=1, device_id=(row, lax.rem(col + off, COLS)), device_id_type=MESH)

    @pl.when(relay)
    def _():
        @pl.loop(0, ROWS)
        def _(r):
            @pl.when(jnp.logical_not(jnp.logical_and(diagonal, r == row)))
            def _():
                pl.semaphore_signal(
                    barrier, inc=1, device_id=(r, (row // 2) * 4 + along), device_id_type=MESH
                )

    load_pf = pltpu.make_async_copy(pf_hbm, pf, mem.at[0])
    load_ct = pltpu.make_async_copy(ct_hbm, ct, mem.at[1])
    load_pf.start()
    load_ct.start()

    eye = identity(128)
    proj[0:32, :] = wleft[...]
    proj[32:64, :] = wright[...]
    half[...] = (shrink_ref[...].astype(F32) * 0.5).astype(BF16)
    for n in range(2):
        lanes = pl.ds(128 * n, 128)
        wide[pl.ds(768 * n, 768), :] = a_ref[:, lanes].astype(F32)
        for r in range(48):
            x_ref[r, :, lanes] = wide[pl.ds(768 * n + r, 16, stride=48), :].astype(BF16)
    wf[...] = w_ref[...].astype(F32)
    wbd[...] = jnp.zeros_like(wbd)
    for e in range(FACTOR):
        block = wf[pl.ds(e, FACTOR, stride=FACTOR), :].astype(BF16)
        for q in range(4):
            wbd[pl.ds(e * 128 + q * 32, 32), pl.ds(q * 128, 128)] = block
    gacc[...] = jnp.zeros_like(gacc)

    pl.semaphore_wait(barrier, ROWS - 1 + COLS - 1 + 4 - jnp.where(diagonal, 1, 0))

    def x_copy(t, peer, slot):
        return pltpu.make_async_remote_copy(
            src_ref=x_ref.at[pl.ds(6 * peer + 2 * t, 2)],
            dst_ref=xbuf.at[pl.ds(2 * t, 2), pl.ds(pl.multiple_of(16 * slot, 16), 16)],
            send_sem=xs.at[t, peer],
            recv_sem=xr.at[t, slot],
            device_id=(peer, col),
            device_id_type=MESH,
        )

    @pl.loop(0, STAGES)
    def _(t):
        @pl.loop(1, ROWS)
        def _(off):
            x_copy(t, lax.rem(row + off, ROWS), row).start()

        xbuf[pl.ds(2 * t, 2), pl.ds(pl.multiple_of(16 * row, 16), 16)] = x_ref[pl.ds(6 * row + 2 * t, 2)]

    def l_copy(t, x, source):
        return pltpu.make_async_remote_copy(
            src_ref=lsend.at[t],
            dst_ref=ltbuf.at[t, half_of_col * ROWS + source],
            send_sem=ls.at[t, x],
            recv_sem=lr.at[t, source],
            device_id=(owner, x * 4 + along),
            device_id_type=MESH,
        )

    def pass_copy(t, half_index, z):
        part = ltbuf.at[t, pl.ds(pl.multiple_of(half_index * ROWS, ROWS), ROWS)]
        return pltpu.make_async_remote_copy(
            src_ref=part,
            dst_ref=part,
            send_sem=ms.at[t, z],
            recv_sem=mr.at[t, half_index],
            device_id=(row, across * 4 + z),
            device_id_type=MESH,
        )

    def send_left(t):
        @pl.when(jnp.logical_not(diagonal))
        def _():
            l_copy(t, across, row).start()

        @pl.when(diagonal)
        def _():
            ltbuf[t, half_of_col * ROWS + row] = lsend[t]

        @pl.loop(1, 4)
        def _(off):
            l_copy(t, lax.rem(across + off, 4), row).start()

    def pass_left(t):
        @pl.when(relay)
        def _():
            @pl.loop(0, ROWS)
            def _(r):
                @pl.when(jnp.logical_not(jnp.logical_and(diagonal, r == row)))
                def _():
                    l_copy(t, across, r).wait_recv()

            @pl.loop(1, 4)
            def _(off):
                pass_copy(t, half_of_col, lax.rem(along + off, 4)).start()

    def r_copy(t, peer, slot):
        return pltpu.make_async_remote_copy(
            src_ref=rsend.at[t],
            dst_ref=rtbuf.at[pl.ds(6 * slot + 2 * t, 2)],
            send_sem=rs.at[t, peer],
            recv_sem=rr.at[t, slot],
            device_id=(peer, col),
            device_id_type=MESH,
        )

    @pl.loop(0, STAGES)
    def _(t):
        @pl.loop(1, ROWS)
        def _(off):
            peer = lax.rem(row + off, ROWS)
            x_copy(t, peer, peer).wait_recv()

        new = attend(
            xbuf[pl.ds(2 * t, 2)], wq[...], wk[...], wv[...], wg[...], gate_bias[...], wo[...]
        )
        ubuf[pl.ds(2 * t, 2)] = new.reshape(2, SEQ, 256)
        factors = dot_nt(proj[...], layer_normalise(new.astype(F32)).astype(BF16))
        left = factors[:32].astype(BF16)
        right = (factors[32:] * (1.0 / SEQ)).astype(BF16)
        for n in range(2):
            lsend[t, n] = left[:, n * SEQ : (n + 1) * SEQ]
            rsend[t, n] = right[:, n * SEQ : (n + 1) * SEQ]

        @pl.loop(1, ROWS)
        def _(off):
            r_copy(t, lax.rem(row + off, ROWS), row).start()

        rtbuf[pl.ds(6 * row + 2 * t, 2)] = rsend[t]

        send_left(t)

        @pl.when(t > 0)
        def _():
            pass_left(t - 1)

    def u_copy(peer, slot):
        return pltpu.make_async_remote_copy(
            src_ref=ubuf.at[:, pl.ds(pl.multiple_of(16 * peer, 16), 16)],
            dst_ref=urecv.at[pl.ds(6 * slot, 6)],
            send_sem=us.at[peer],
            recv_sem=ur.at[slot],
            device_id=(peer, col),
            device_id_type=MESH,
        )

    @pl.loop(1, ROWS)
    def _(off):
        u_copy(lax.rem(row + off, ROWS), row).start()

    urecv[pl.ds(6 * row, 6)] = ubuf[:, pl.ds(pl.multiple_of(16 * row, 16), 16)]

    @pl.loop(0, STAGES)
    def _(t):
        @pl.loop(1, ROWS)
        def _(off):
            peer = lax.rem(row + off, ROWS)
            r_copy(t, peer, peer).wait_recv()

    pass_left(STAGES - 1)

    for j in range(N_J):
        rtf[pl.ds(j, FACTOR, stride=N_J), :] = rtbuf[j].astype(F32)
    rt[...] = rtf[...].astype(BF16)
    r2[...] = dot_nt(eye, rt[...]).astype(BF16)
    load_pf.wait()
    load_ct.wait()

    def gl_copy(q, target, source):
        return pltpu.make_async_remote_copy(
            src_ref=glsend.at[q, target],
            dst_ref=glrecv.at[q, source],
            send_sem=gs.at[q, target],
            recv_sem=gr_sem.at[q, source],
            device_id=(row, target),
            device_id_type=MESH,
        )

    def store_copy(q):
        part = (slice(None), pl.ds(2 * q, 2))
        return pltpu.make_async_copy(out.at[part], out_hbm.at[part], mem.at[3 + q])

    def gr_copy(peer, slot):
        return pltpu.make_async_remote_copy(
            src_ref=grsend.at[peer],
            dst_ref=grrecv.at[slot],
            send_sem=hs.at[peer],
            recv_sem=hr.at[slot],
            device_id=(peer, col),
            device_id_type=MESH,
        )

    @pl.loop(0, STAGES)
    def _(q):
        for n in range(2):
            @pl.when(jnp.logical_not(jnp.logical_and(relay, half_of_col == n)))
            def _():
                pass_copy(q, n, along).wait_recv()

        lt = ltbuf[q].reshape(N_I * FACTOR, SEQ)

        for eb in range(4):
            o = dot_nt(rt[pl.ds(eb * 384, 384), :], lt).astype(BF16)
            for e in range(8):
                for g in range(N_G):
                    osc[pl.ds(g * N_J, N_J), pl.ds(eb * 1024 + e * 128, 128)] = o[
                        e * N_J : (e + 1) * N_J, g * 128 : (g + 1) * 128
                    ]

        mid[...] = dot_nn(osc[...], wbd[...])

        @pl.loop(0, N_G // 4)
        def _(outer_step):
            for inner in range(2):
                g0 = (outer_step * 2 + inner) * 2
                blocks = [mid[pl.ds(pl.multiple_of((g0 + k) * N_J, N_J), N_J), :] for k in range(2)]
                x = jnp.concatenate(
                    [block[:, n * 128 : (n + 1) * 128] for block in blocks for n in range(4)], axis=0
                )
                part = (pl.ds(g0 * 2, 4), pl.ds(q * 2, 2))
                cot = ct[part].reshape(8 * N_J, PAIR_W)
                x = pf[part].reshape(8 * N_J, PAIR_W) + x + bias_ref[...]
                result, back = transition(x, cot, expand_ref[...], half[...])
                out[part] = result.reshape(4, 2, N_J, PAIR_W)
                back = back.astype(BF16)
                for k in range(2):
                    for n in range(4):
                        bmsc[pl.ds(pl.multiple_of((g0 + k) * N_J, N_J), N_J), pl.ds(n * 128, 128)] = back[
                            (4 * k + n) * N_J : (4 * k + n + 1) * N_J, :
                        ]

        store_copy(q).start()

        for eb in range(4):
            b = dot_nt(bmsc[...], wbd[pl.ds(eb * 1024, 1024), :]).astype(BF16)
            for e in range(8):
                for g in range(N_G):
                    bsc[pl.ds(eb * 384 + e * N_J, N_J), pl.ds(g * 128, 128)] = b[
                        g * N_J : (g + 1) * N_J, e * 128 : (e + 1) * 128
                    ]

        gacc[...] += dot_nt(dot_nt(eye, lt).astype(BF16), bsc[...])

        @pl.when(q == STAGES - 1)
        def _():
            scaled = (gacc[...] * (1.0 / SEQ)).astype(BF16)
            rtf[...] = lax.dot_general(
                scaled, eye, (((0,), (0,)), ((), ())), preferred_element_type=F32
            )
            by_residue = jnp.concatenate(
                [rtf[pl.ds(j, FACTOR, stride=N_J), :] for j in range(N_J)], axis=0
            )
            grt = dot_nt(eye, by_residue.astype(BF16)).astype(BF16)
            for d in range(ROWS):
                grsend[d] = grt[16 * d : 16 * d + 16]

            @pl.loop(1, ROWS)
            def _(off):
                gr_copy(lax.rem(row + off, ROWS), row).start()

        gl = dot_nn(r2[...], bsc[...])
        for d in range(COLS):
            part = gl[8 * d : 8 * d + 8]
            glsend[q, d] = jnp.concatenate([part[:, :512], part[:, 512:]], axis=0).astype(BF16)

        @pl.loop(1, COLS)
        def _(off):
            gl_copy(q, lax.rem(col + off, COLS), col).start()

    @pl.loop(1, ROWS)
    def _(off):
        peer = lax.rem(row + off, ROWS)
        u_copy(peer, peer).wait_recv()

    for n in range(2):
        lanes = pl.ds(128 * n, 128)
        for r in range(48):
            wide[pl.ds(768 * n + r, 16, stride=48), :] = urecv[r, :, lanes].astype(F32)
        upd_ref[:, lanes] = wide[pl.ds(768 * n, 768), :].astype(BF16)

    sums = []
    for q in range(STAGES):
        glrecv[q, col] = glsend[q, col]

        @pl.loop(1, COLS)
        def _(off):
            source = lax.rem(col + off, COLS)
            gl_copy(q, source, source).wait_recv()

        total = glrecv[q, 0].astype(F32)
        for n in range(1, COLS):
            total = total + glrecv[q, n].astype(F32)
        sums.append(total)
    for half_of in range(2):
        pieces = [
            sums[q][8 * half_of : 8 * half_of + 8, 64 * n : 64 * n + 64] for n in range(8) for q in range(STAGES)
        ]
        gl_ref[:, pl.ds(1536 * half_of, 1536)] = jnp.concatenate(pieces, axis=1)

    grrecv[row] = grsend[row]

    @pl.loop(1, ROWS)
    def _(off):
        peer = lax.rem(row + off, ROWS)
        gr_copy(peer, peer).wait_recv()

    total = jnp.zeros((16, N_J * FACTOR), F32)
    for s in range(ROWS):
        total = total + grrecv[s].astype(F32)
    gr_ref[...] = total

    @pl.loop(1, ROWS)
    def _(off):
        peer = lax.rem(row + off, ROWS)
        u_copy(peer, row).wait_send()
        gr_copy(peer, row).wait_send()

    @pl.loop(0, STAGES)
    def _(t):
        store_copy(t).wait()

        @pl.loop(1, ROWS)
        def _(off):
            peer = lax.rem(row + off, ROWS)
            x_copy(t, peer, row).wait_send()
            r_copy(t, peer, row).wait_send()

        @pl.when(jnp.logical_not(diagonal))
        def _():
            l_copy(t, across, row).wait_send()

        @pl.loop(1, 4)
        def _(off):
            l_copy(t, lax.rem(across + off, 4), row).wait_send()

            @pl.when(relay)
            def _():
                pass_copy(t, half_of_col, lax.rem(along + off, 4)).wait_send()

        @pl.loop(1, COLS)
        def _(off):
            gl_copy(t, lax.rem(col + off, COLS), col).wait_send()


def hand_over(out_in, upd_in, gl_in, gr_in, out_to, upd_to, gl_to, gr_to, out_v, upd_v, gl_v, gr_v, sems):
    jobs = []
    for n in range(4):
        part = pl.ds(4 * n, 4)
        jobs.append((out_in.at[part], out_v.at[part], out_to.at[part]))
    jobs += [(upd_in, upd_v, upd_to), (gl_in, gl_v, gl_to), (gr_in, gr_v, gr_to)]
    first = [pltpu.make_async_copy(a, b, sems.at[0, n]) for n, (a, b, c) in enumerate(jobs)]
    second = [pltpu.make_async_copy(b, c, sems.at[1, n]) for n, (a, b, c) in enumerate(jobs)]
    for copy in first:
        copy.start()
    for a, b in zip(first, second):
        a.wait()
        b.start()
    for copy in second:
        copy.wait()


def local(
    alignment, pair_features, query_weight, key_weight, value_projection, gate_projection,
    gate_bias, output_projection, left_projection, right_projection, outer_weight, outer_bias,
    expand_weight, shrink_weight, cotangent,
):
    vmem = pl.BlockSpec(memory_space=pltpu.VMEM)
    hbm = pl.BlockSpec(memory_space=pl.ANY)
    dma = pltpu.SemaphoreType.DMA
    upd, out, gl, gr = pl.pallas_call(
        kernel,
        in_specs=[vmem] * 13 + [hbm] * 2,
        out_specs=[vmem, hbm, vmem, vmem],
        out_shape=[
            jax.ShapeDtypeStruct((16 * 48, 256), BF16),
            jax.ShapeDtypeStruct((16, 6, N_J, PAIR_W), F32),
            jax.ShapeDtypeStruct((8, 3072), F32),
            jax.ShapeDtypeStruct((16, N_J * FACTOR), F32),
        ],
        scratch_shapes=[
            pltpu.VMEM((2 * 16 * 48, 128), F32),
            pltpu.VMEM((48, 16, 256), BF16),
            pltpu.VMEM((6, SEQ, 256), BF16),
            pltpu.VMEM((6, SEQ, 256), BF16),
            pltpu.VMEM((48, 16, 256), BF16),
            pltpu.VMEM((512, PAIR_W), BF16),
            pltpu.VMEM((64, 256), BF16),
            pltpu.VMEM((STAGES, 2, FACTOR, SEQ), BF16),
            pltpu.VMEM((STAGES, 2, FACTOR, SEQ), BF16),
            pltpu.VMEM((STAGES, 16, 2, FACTOR, SEQ), BF16),
            pltpu.VMEM((N_J, FACTOR, SEQ), BF16),
            pltpu.VMEM((FACTOR * N_J, SEQ), F32),
            pltpu.VMEM((FACTOR * N_J, SEQ), BF16),
            pltpu.VMEM((SEQ, FACTOR * N_J), BF16),
            pltpu.VMEM((FACTOR * FACTOR, PAIR_W), F32),
            pltpu.VMEM((4096, 512), BF16),
            pltpu.VMEM((16, 6, N_J, PAIR_W), F32),
            pltpu.VMEM((16, 6, N_J, PAIR_W), F32),
            pltpu.VMEM((16, 6, N_J, PAIR_W), F32),
            pltpu.VMEM((N_G * N_J, 4096), BF16),
            pltpu.VMEM((N_G * N_J, 512), F32),
            pltpu.VMEM((N_G * N_J, 512), BF16),
            pltpu.VMEM((FACTOR * N_J, 1024), BF16),
            pltpu.VMEM((SEQ, FACTOR * N_J), F32),
            pltpu.VMEM((STAGES, COLS, 16, 512), BF16),
            pltpu.VMEM((STAGES, COLS, 16, 512), BF16),
            pltpu.VMEM((ROWS, 16, N_J * FACTOR), BF16),
            pltpu.VMEM((ROWS, 16, N_J * FACTOR), BF16),
            dma((STAGES, ROWS)), dma((STAGES, ROWS)),
            dma((STAGES, 4)), dma((STAGES, ROWS)),
            dma((STAGES, 4)), dma((STAGES, 2)),
            dma((STAGES, ROWS)), dma((STAGES, ROWS)),
            dma((ROWS,)), dma((ROWS,)),
            dma((STAGES, COLS)), dma((STAGES, COLS)),
            dma((ROWS,)), dma((ROWS,)),
            dma((6,)),
        ],
        compiler_params=pltpu.CompilerParams(
            collective_id=0, has_side_effects=True, vmem_limit_bytes=60 * 1024 * 1024
        ),
        name="block",
    )(
        alignment.reshape(16 * 48, 256), query_weight, key_weight, value_projection, gate_projection,
        gate_bias.reshape(1, -1), output_projection, left_projection.T, right_projection.T,
        outer_weight, outer_bias.reshape(1, -1), expand_weight, shrink_weight,
        pair_features.reshape(16, 6, N_J, PAIR_W), cotangent.reshape(16, 6, N_J, PAIR_W),
    )
    results = (out, upd, gl, gr)
    out, upd, gl, gr = pl.pallas_call(
        hand_over,
        in_specs=[hbm] * 4,
        out_specs=[hbm] * 4,
        out_shape=[jax.ShapeDtypeStruct(a.shape, a.dtype) for a in results],
        scratch_shapes=[pltpu.VMEM(a.shape, a.dtype) for a in results] + [dma((2, 7))],
        name="hand_over",
    )(*results)
    return upd.reshape(16, 48, 256), out.reshape(96, N_J, PAIR_W), gl, gr


def solution(mesh):
    return jax.shard_map(
        local,
        mesh=mesh,
        in_specs=(P("row", "col", None), P("row", "col", None)) + (P(),) * 12 + (P("row", "col", None),),
        out_specs=(P("row", "col", None), P("row", "col", None), P("col", "row"), P("row", "col")),
        check_vma=False,
    )
```
